32 devices in a mesh: groups: 2 (over y), seq: 8 (over z, x), heads: 2 (over core).
Axes of the slice: x: 2, y: 2, z: 4, core: 2. Of those that a mesh axis runs over, the one named last changes fastest.
Arguments:
- queries: bfloat16 [2048, 32, 128], P(('groups', 'seq'), 'heads'), parts along dimension 0, may hold values from -6 to 6
- keys: bfloat16 [2048, 32, 128], P(('groups', 'seq'), 'heads'), parts along dimension 0, may hold values from -6 to 6
- values: bfloat16 [2048, 32, 128], P(('groups', 'seq'), 'heads'), parts along dimension 0, may hold values from -6 to 6
- w_query: bfloat16 [32, 128, 128], P('heads'), may hold values from -1 to 1
- w_key: bfloat16 [32, 128, 128], P('heads'), may hold values from -1 to 1
Outputs:
- student_out: bfloat16 [2048, 32, 128], P(('groups', 'seq'), 'heads'), parts along dimension 0
- grad_query: float32 [64, 128, 128], P(('groups', 'heads')), parts along dimension 0
- grad_key: float32 [64, 128, 128], P(('groups', 'heads')), parts along dimension 0
The draws below stay inside these ranges and needn't reach their ends.
There are 2 independent parts, one for each index of `groups`. The reference program is written for one: setup_inputs(seed, part) draws one part's arguments, and reference() takes and returns one part's arrays. A program takes and returns all parts, laid end to end along the dimension named above; an argument that names none is the same for every part. Nothing has to cross between parts.
All inputs are finite; a program needn't handle non-finite values.
Results may differ from the reference program's by a relative error of at most 0.0064.
Values may be sent and summed in bfloat16 or wider, within the bound.
A program may use at most 128 MiB of HBM per device.

```python
import math
import jax
import jax.numpy as jnp
from jax import lax

HEADS = 32
HD = 128
FEAT = 256
BLOCK = 128
LENGTH = 1024


def drawn_pair(key):
    base = jax.random.fold_in(key, 7301)
    query_seed, key_seed = jax.random.split(base, 2)
    shape = (LENGTH, HEADS, HD)
    queries = jnp.clip(1.5 * jax.random.normal(query_seed, shape, jnp.float32), -6.0, 6.0)
    keys = jnp.clip(1.5 * jax.random.normal(key_seed, shape, jnp.float32), -6.0, 6.0)
    return (queries, keys)


def draw_queries(key, part):
    return drawn_pair(key)[0].astype(jnp.bfloat16)


def draw_keys(key, part):
    return drawn_pair(key)[1].astype(jnp.bfloat16)


def block_scale(stream_key, extent, cuts, smallest, high):
    loudness, own = 1.0, jax.random.fold_in(stream_key, 6)
    for dim, parts in cuts:
        draws = jnp.exp(jax.random.uniform(jax.random.fold_in(own, dim), (parts,), jnp.float32, smallest / len(cuts), high / len(cuts)))
        loudness = loudness * jnp.repeat(draws, extent[dim] // parts).reshape([-1 if axis == dim else 1 for axis in range(len(extent))])
    return loudness


def gaussian(key, shape, scale, reach, shards=(), kind=jnp.bfloat16):
    values = jax.random.normal(key, shape, jnp.float32) * scale
    if len(shards) > 0:
        values = block_scale(key, shape, shards, -0.22, 0.18) * values
    return jnp.clip(values, min=-reach, max=reach).astype(kind)


def setup_inputs(seed: int = 0, part: int = 0) -> dict:
    streams_of = jax.random.split(jax.random.key(seed), 6)
    part_splits = jax.random.split(jax.random.fold_in(streams_of[5], part), 6)
    queries = draw_queries(jax.random.fold_in(jax.random.fold_in(streams_of[5], part), 71), part)
    keys = draw_keys(jax.random.fold_in(jax.random.fold_in(streams_of[5], part), 71), part)
    values = gaussian(part_splits[2], (LENGTH, HEADS, HD), 1.0, 6.0, ((0, 8), (1, 2)))
    w_query = gaussian(streams_of[3], (HEADS, HD, HD), 0.18, 1.0, ((0, 2),))
    w_key = gaussian(streams_of[4], (HEADS, HD, HD), 0.18, 1.0, ((0, 2),))
    return {"queries": queries, "keys": keys, "values": values, "w_query": w_query, "w_key": w_key}


HIGHEST = lax.Precision.HIGHEST

def product(form, left, right):
    return jnp.einsum(form, left.astype(jnp.float32), right.astype(jnp.float32), precision=HIGHEST)

def rounded(array):
    return lax.optimization_barrier(array.astype(jnp.bfloat16))

def teacher_head(query, key_rows, value_rows):
    length = query.shape[0]
    width = query.shape[1]
    rows = min(512, length)

    def one_block(index):
        block_query = lax.dynamic_slice_in_dim(query, index * rows, rows, 0)
        scores = product('qd,kd->qk', block_query, key_rows) / math.sqrt(width)
        position = index * rows + jnp.arange(rows, dtype=jnp.int32)
        allowed = jnp.arange(length, dtype=jnp.int32)[None, :] <= position[:, None]
        scores = jnp.where(allowed, scores, -1e+30)
        top = lax.optimization_barrier(jnp.max(scores, 1, keepdims=True))
        weights = jnp.where(allowed, jnp.exp(scores - top), 0.0)
        summed = product('qk,kd->qd', rounded(weights), value_rows)
        return (summed / lax.optimization_barrier(jnp.sum(weights, 1, keepdims=True))).astype(jnp.bfloat16)
    blocks = lax.map(one_block, jnp.arange(length // rows, dtype=jnp.int32))
    return blocks.reshape(length, width)

def feature_halves(inputs, weight):
    mixed = product('td,de->te', inputs, weight)
    upper = jnp.exp(mixed)
    lower = jnp.exp(-mixed)
    return (upper / lax.optimization_barrier(jnp.sum(upper, -1, keepdims=True)), lower / lax.optimization_barrier(jnp.sum(lower, -1, keepdims=True)))

def feature_weight_grad(plus, minus, grad_feat, inputs):
    width = plus.shape[-1]
    grad_plus = grad_feat[:, :width]
    grad_minus = grad_feat[:, width:]
    grad_mixed = plus * (grad_plus - lax.optimization_barrier(jnp.sum(plus * grad_plus, -1, keepdims=True)))
    grad_mixed = grad_mixed - minus * (grad_minus - lax.optimization_barrier(jnp.sum(minus * grad_minus, -1, keepdims=True)))
    return product('td,te->de', inputs, grad_mixed)

def student_pass(query_feat, key_feat, values, teacher, allowed, states, sums):
    scores = jnp.where(allowed, product('nqhf,nkhf->nhqk', query_feat, key_feat), 0.0)
    state_low = rounded(states)
    numer = product('nhqk,nkhd->nqhd', rounded(scores), values) + product('nqhf,nhfd->nqhd', query_feat, state_low)
    denom = jnp.transpose(lax.optimization_barrier(jnp.sum(scores, -1)), (0, 2, 1)) + lax.optimization_barrier(jnp.sum(query_feat.astype(jnp.float32) * sums[:, None], -1))
    student = numer / denom[..., None]
    diff = student - teacher.astype(jnp.float32)
    grad_numer = rounded(diff / denom[..., None])
    grad_denom = -lax.optimization_barrier(jnp.sum(diff * student, -1)) / denom
    link = product('nqhd,nkhd->nhqk', grad_numer, values)
    link = rounded(jnp.where(allowed, link + jnp.transpose(grad_denom, (0, 2, 1))[..., None], 0.0))
    grad_query = product('nhqk,nkhf->nqhf', link, key_feat) + product('nqhd,nhfd->nqhf', grad_numer, state_low)
    grad_query = grad_query + grad_denom[..., None] * sums[:, None]
    back_state = product('nqhf,nqhd->nhfd', query_feat, grad_numer)
    back_sum = lax.optimization_barrier(jnp.sum(query_feat.astype(jnp.float32) * grad_denom[..., None], 1))
    key_inner = product('nhqk,nqhf->nkhf', link, query_feat)
    return (student, grad_query, key_inner, back_state, back_sum)

def before_sums(terms):
    return jnp.concatenate([jnp.zeros_like(terms[:1]), jnp.cumsum(terms, 0)[:-1]], 0)

def after_sums(terms):
    return jnp.concatenate([jnp.cumsum(terms[::-1], 0)[::-1][1:], jnp.zeros_like(terms[:1])], 0)

def student_head(query, key_rows, value_rows, teacher, weight_query, weight_key):
    blocks = LENGTH // BLOCK
    query_plus, query_minus = feature_halves(query, weight_query)
    key_plus, key_minus = feature_halves(key_rows, weight_key)
    query_feat = rounded(jnp.concatenate([query_plus, query_minus], -1))
    key_feat = rounded(jnp.concatenate([key_plus, key_minus], -1))
    query_blocks = query_feat.reshape(blocks, BLOCK, 1, FEAT)
    key_blocks = key_feat.reshape(blocks, BLOCK, 1, FEAT)
    value_blocks = value_rows.reshape(blocks, BLOCK, 1, HD)
    teacher_blocks = teacher.reshape(blocks, BLOCK, 1, HD)
    key_state = product('nkhf,nkhd->nhfd', key_blocks, value_blocks)
    key_sum = lax.optimization_barrier(jnp.sum(key_blocks.astype(jnp.float32), 1))
    position = jnp.arange(BLOCK, dtype=jnp.int32)
    allowed = position[None, :] <= position[:, None]
    student, grad_query, key_inner, back_state, back_sum = student_pass(query_blocks, key_blocks, value_blocks, teacher_blocks, allowed, before_sums(key_state), before_sums(key_sum))
    grad_key = key_inner + product('nkhd,nhfd->nkhf', value_blocks, after_sums(back_state)) + after_sums(back_sum)[:, None]
    query_grad = feature_weight_grad(query_plus, query_minus, grad_query.reshape(LENGTH, FEAT), query)
    key_grad = feature_weight_grad(key_plus, key_minus, grad_key.reshape(LENGTH, FEAT), key_rows)
    return (student.reshape(LENGTH, HD).astype(jnp.bfloat16), query_grad, key_grad)

def reference(queries, keys, values, w_query, w_key):

    def one_head(index):
        query = lax.dynamic_index_in_dim(queries, index, 1, keepdims=False)
        key_rows = lax.dynamic_index_in_dim(keys, index, 1, keepdims=False)
        value_rows = lax.dynamic_index_in_dim(values, index, 1, keepdims=False)
        weight_query = lax.dynamic_index_in_dim(w_query, index, 0, keepdims=False)
        weight_key = lax.dynamic_index_in_dim(w_key, index, 0, keepdims=False)
        teacher = teacher_head(query, key_rows, value_rows)
        return student_head(query, key_rows, value_rows, teacher, weight_query, weight_key)
    results = lax.map(one_head, jnp.arange(HEADS, dtype=jnp.int32))
    student_out = jnp.moveaxis(results[0], 0, 1)
    return (student_out, results[1], results[2])
```

```python
import functools
import math

import jax
import jax.numpy as jnp
from jax import lax
from jax.experimental import pallas as pl
from jax.experimental.pallas import tpu as pltpu
from jax.sharding import PartitionSpec as P

HIGHEST = lax.Precision.HIGHEST


def passed_along(value, axis, steps):
    count = lax.axis_size(axis)
    pairs = [(source, (source + steps) % count) for source in range(count)]
    return lax.ppermute(value, axis, pairs)


def teacher_head(query, key_rows, value_rows, residue, spread):
    rows = query.shape[0]
    length = key_rows.shape[0]
    width = query.shape[1]
    query_block = min(512, rows)
    key_block = min(512, length)
    key_blocks = length // key_block
    scale = 1.0 / math.sqrt(width)

    def one_block(index):
        block_query = lax.dynamic_slice_in_dim(query, index * query_block, query_block, 0)
        position = (
            index * query_block + jnp.arange(query_block, dtype=jnp.int32)
        ) * spread + residue
        limit = (index + 1) * query_block * spread
        needed = jnp.minimum(key_blocks, (limit + key_block - 1) // key_block)

        def visit(inner, carry):
            top, total, summed = carry
            block_key = lax.dynamic_slice_in_dim(key_rows, inner * key_block, key_block, 0)
            block_value = lax.dynamic_slice_in_dim(value_rows, inner * key_block, key_block, 0)
            scores = (
                jnp.einsum("qd,kd->qk", block_query, block_key, preferred_element_type=jnp.float32)
                * scale
            )
            key_position = inner * key_block + jnp.arange(key_block, dtype=jnp.int32)
            scores = jnp.where(key_position[None, :] <= position[:, None], scores, -1e30)
            new_top = jnp.maximum(top, jnp.max(scores, 1))
            factor = jnp.exp(top - new_top)
            weights = jnp.exp(scores - new_top[:, None])
            total = total * factor + jnp.sum(weights, 1)
            summed = summed * factor[:, None] + jnp.dot(
                weights.astype(jnp.bfloat16), block_value, preferred_element_type=jnp.float32
            )
            return (new_top, total, summed)

        start = (
            jnp.full((query_block,), -1e30, jnp.float32),
            jnp.zeros((query_block,), jnp.float32),
            jnp.zeros((query_block, width), jnp.float32),
        )
        top, total, summed = lax.fori_loop(0, needed, visit, start)
        return (summed / total[:, None]).astype(jnp.bfloat16)

    blocks = lax.map(one_block, jnp.arange(rows // query_block, dtype=jnp.int32))
    return blocks.reshape(rows, width)


def feature_halves(inputs, weight):
    mixed = jnp.einsum("thd,hde->the", inputs, weight, preferred_element_type=jnp.float32)
    upper = jnp.exp(mixed)
    lower = jnp.exp(-mixed)
    return (upper / jnp.sum(upper, -1, keepdims=True), lower / jnp.sum(lower, -1, keepdims=True))


def feature_weight_grad(plus, minus, grad_feat, inputs):
    width = plus.shape[-1]
    grad_plus = grad_feat[..., :width]
    grad_minus = grad_feat[..., width:]
    grad_mixed = plus * (grad_plus - jnp.sum(plus * grad_plus, -1, keepdims=True))
    grad_mixed = grad_mixed - minus * (grad_minus - jnp.sum(minus * grad_minus, -1, keepdims=True))
    return jnp.einsum("thd,the->hde", inputs.astype(jnp.float32), grad_mixed, precision=HIGHEST)


def student_pass(query_feat, key_feat, values, teacher, allowed, states, sums):
    scores = jnp.einsum("nqhf,nkhf->nhqk", query_feat, key_feat, preferred_element_type=jnp.float32)
    scores = jnp.where(allowed, scores, 0.0)
    state_low = states.astype(jnp.bfloat16)
    numer = jnp.einsum(
        "nhqk,nkhd->nqhd", scores.astype(jnp.bfloat16), values, preferred_element_type=jnp.float32
    )
    numer = numer + jnp.einsum(
        "nqhf,nhfd->nqhd", query_feat, state_low, preferred_element_type=jnp.float32
    )
    denom = jnp.transpose(jnp.sum(scores, -1), (0, 2, 1)) + jnp.sum(
        query_feat.astype(jnp.float32) * sums[:, None], -1
    )
    student = numer / denom[..., None]
    diff = student - teacher.astype(jnp.float32)
    grad_numer = (diff / denom[..., None]).astype(jnp.bfloat16)
    grad_denom = -jnp.sum(diff * student, -1) / denom
    link = jnp.einsum("nqhd,nkhd->nhqk", grad_numer, values, preferred_element_type=jnp.float32)
    link = jnp.where(allowed, link + jnp.transpose(grad_denom, (0, 2, 1))[..., None], 0.0).astype(
        jnp.bfloat16
    )
    grad_query = jnp.einsum("nhqk,nkhf->nqhf", link, key_feat, preferred_element_type=jnp.float32)
    grad_query = grad_query + jnp.einsum(
        "nqhd,nhfd->nqhf", grad_numer, state_low, preferred_element_type=jnp.float32
    )
    grad_query = grad_query + grad_denom[..., None] * sums[:, None]
    back_state = jnp.einsum(
        "nqhf,nqhd->nhfd", query_feat, grad_numer, preferred_element_type=jnp.float32
    )
    back_sum = jnp.sum(query_feat.astype(jnp.float32) * grad_denom[..., None], 1)
    key_inner = jnp.einsum("nhqk,nqhf->nkhf", link, query_feat, preferred_element_type=jnp.float32)
    return (student, grad_query, key_inner, back_state, back_sum)


def on_device_shared(queries, keys, values, w_query, w_key):
    block, heads, width = queries.shape
    seqs = lax.axis_size("seq")
    here = lax.axis_index("seq")
    spread = max(1, seqs // heads)
    items = spread * heads // seqs
    residue = here * items // heads
    query_rows = queries.reshape(block // spread, spread * heads, width)
    key_rows = jnp.broadcast_to(keys[:, None], (block, spread, heads, width)).reshape(
        block, spread * heads, width
    )
    value_rows = jnp.broadcast_to(values[:, None], (block, spread, heads, width)).reshape(
        block, spread * heads, width
    )
    query_items, key_items, value_items = (
        lax.all_to_all(query_rows, "seq", split_axis=1, concat_axis=0, tiled=True),
        lax.all_to_all(key_rows, "seq", split_axis=1, concat_axis=0, tiled=True),
        lax.all_to_all(value_rows, "seq", split_axis=1, concat_axis=0, tiled=True),
    )

    def teach(group):
        return teacher_head(group[0], group[1], group[2], residue, spread)

    teacher_items = lax.map(
        teach,
        (
            jnp.moveaxis(query_items, 1, 0),
            jnp.moveaxis(key_items, 1, 0),
            jnp.moveaxis(value_items, 1, 0),
        ),
    )
    teacher_items = jnp.moveaxis(teacher_items, 0, 1)
    first = here * items % heads
    part_query = lax.dynamic_slice_in_dim(w_query, first, items, 0)
    part_key = lax.dynamic_slice_in_dim(w_key, first, items, 0)
    query_plus, query_minus = feature_halves(query_items, part_query)
    key_plus, key_minus = feature_halves(key_items, part_key)
    query_feat = jnp.concatenate([query_plus, query_minus], -1).astype(jnp.bfloat16)
    key_feat = jnp.concatenate([key_plus, key_minus], -1).astype(jnp.bfloat16)
    feat = 2 * width
    query_blocks = query_feat.reshape(seqs, block // spread, items, feat)
    key_blocks = key_feat.reshape(seqs, block, items, feat)
    value_blocks = value_items.reshape(seqs, block, items, width)
    teacher_blocks = teacher_items.reshape(seqs, block // spread, items, width)
    key_state = jnp.einsum(
        "nkhf,nkhd->nhfd", key_blocks, value_blocks, preferred_element_type=jnp.float32
    )
    key_sum = jnp.sum(key_blocks.astype(jnp.float32), 1)
    before_state = jnp.concatenate(
        [jnp.zeros_like(key_state[:1]), jnp.cumsum(key_state, 0)[:-1]], 0
    )
    before_sum = jnp.concatenate([jnp.zeros_like(key_sum[:1]), jnp.cumsum(key_sum, 0)[:-1]], 0)
    query_place = jnp.arange(block // spread, dtype=jnp.int32)
    key_place = jnp.arange(block, dtype=jnp.int32)
    allowed = key_place[None, :] <= query_place[:, None] * spread + residue
    student, grad_query, key_inner, back_state, back_sum = student_pass(
        query_blocks, key_blocks, value_blocks, teacher_blocks, allowed, before_state, before_sum
    )
    after_state = jnp.concatenate(
        [jnp.cumsum(back_state[::-1], 0)[::-1][1:], jnp.zeros_like(back_state[:1])], 0
    )
    after_sum = jnp.concatenate(
        [jnp.cumsum(back_sum[::-1], 0)[::-1][1:], jnp.zeros_like(back_sum[:1])], 0
    )
    grad_key = key_inner + jnp.einsum(
        "nkhd,nhfd->nkhf", value_blocks.astype(jnp.float32), after_state, precision=HIGHEST
    )
    grad_key = grad_key + after_sum[:, None]
    item_query_grad = feature_weight_grad(
        query_plus, query_minus, grad_query.reshape(-1, items, feat), query_items
    )
    item_key_grad = feature_weight_grad(
        key_plus, key_minus, grad_key.reshape(-1, items, feat), key_items
    )
    student_items = student.reshape(-1, items, width).astype(jnp.bfloat16)
    student_out = lax.all_to_all(
        student_items, "seq", split_axis=0, concat_axis=1, tiled=True
    ).reshape(block, heads, width)
    stride = seqs // spread
    summed_query = item_query_grad
    summed_key = item_key_grad
    for partner in range(1, spread):
        arrived = (
            passed_along(item_query_grad.astype(jnp.bfloat16), "seq", partner * stride).astype(
                item_query_grad.dtype
            ),
            passed_along(item_key_grad.astype(jnp.bfloat16), "seq", partner * stride).astype(
                item_key_grad.dtype
            ),
        )
        summed_query = summed_query + arrived[0]
        summed_key = summed_key + arrived[1]
    portion = width // spread
    owned_query = lax.dynamic_slice_in_dim(summed_query, residue * portion, portion, 1)[None]
    owned_key = lax.dynamic_slice_in_dim(summed_key, residue * portion, portion, 1)[None]
    whole_query, whole_key = (
        lax.all_gather(owned_query, "seq", axis=0, tiled=True),
        lax.all_gather(owned_key, "seq", axis=0, tiled=True),
    )

    def arrange(gathered):
        shaped = gathered.reshape(spread, stride, items, portion, width)
        return jnp.transpose(shaped, (1, 2, 0, 3, 4)).reshape(heads, width, width)

    query_grad = arrange(whole_query)
    key_grad = arrange(whole_key)
    return (student_out, query_grad, key_grad)


MESH = pl.DeviceIdType.MESH


def dot(left, right, dims):
    return lax.dot_general(left, right, (dims, ((), ())), preferred_element_type=jnp.float32)


def dot_nn(left, right):
    return dot(left, right, ((1,), (0,)))


def dot_nt(left, right):
    return dot(left, right, ((1,), (1,)))


def dot_tn(left, right):
    return dot(left, right, ((0,), (0,)))


def two_terms(value):
    high = value.astype(jnp.bfloat16)
    return high, (value - high.astype(jnp.float32)).astype(jnp.bfloat16)


def softmax_back(plus, minus, grad_feat):
    width = plus.shape[-1]
    grad_plus = grad_feat[:, :width]
    grad_minus = grad_feat[:, width:]
    mixed = plus * (grad_plus - jnp.sum(plus * grad_plus, -1, keepdims=True))
    return mixed - minus * (grad_minus - jnp.sum(minus * grad_minus, -1, keepdims=True))


def halves(rows, weight):
    mixed = dot_nn(rows, weight)
    upper = jnp.exp(mixed)
    lower = jnp.exp(-mixed)
    plus = upper * (1.0 / jnp.sum(upper, -1, keepdims=True))
    minus = lower * (1.0 / jnp.sum(lower, -1, keepdims=True))
    return plus, minus


def doubling(count):
    bits = [1 << place for place in reversed(range(count.bit_length() - 1))]
    messages = []
    for level, bit in enumerate(bits):
        masks = [0]
        for higher in bits[:level]:
            masks = masks + [mask + higher for mask in masks]
        messages = messages + [(bit, mask) for mask in masks]
    return bits, messages


def fused_kernel(
    seqs, items,
    q_in, k_in, v_in, wq_ref, wk_ref,
    out_ref, grad_ref,
    q_rows, k_rows, v_rows, q_ref, k_ref, v_ref, qs, ks, vs, wqs, wks, plus_k, minus_k, feat_k, inner, back_state, back_sum,
    state, state_sum, after, after_sum, grad_acc, out_buf, grad_buf,
    send_sem, recv_sem, out_send, out_recv, grad_send, grad_recv,
    local_sem, weight_sem, own_sem, load_sem,
):
    me = lax.axis_index("seq")
    block, width = q_ref.shape[1], q_ref.shape[2]
    step = 2
    chunk = block * step
    chunks = seqs // step
    feat = 2 * width
    bits, messages = doubling(seqs)

    def peer(distance):
        return lax.rem(me + distance, seqs)

    def remote(src, dst, send, recv, device):
        return pltpu.make_async_remote_copy(
            src_ref=src, dst_ref=dst, send_sem=send, recv_sem=recv,
            device_id={"seq": device}, device_id_type=MESH,
        )

    streams = ((q_ref, qs), (k_ref, ks), (v_ref, vs))

    def input_copy(which, item, distance):
        source, landing = streams[which]
        target = peer(distance)
        return remote(
            source.at[target * items + item], landing.at[item, me],
            send_sem.at[which, item, distance], recv_sem.at[which, item, distance], target,
        )

    def own_input(which, item):
        source, landing = streams[which]
        return pltpu.make_async_copy(
            source.at[me * items + item], landing.at[item, me], local_sem.at[which, item]
        )

    def arrived_input(which, item, distance):
        source, landing = streams[which]
        origin = peer(seqs - distance)
        return remote(
            source.at[item], landing.at[item, origin],
            send_sem.at[which, item, distance], recv_sem.at[which, item, distance], origin,
        )

    def out_copy(item, target):
        return remote(
            out_buf.at[item, target], out_ref.at[me * items + item],
            out_send.at[item, target], out_recv.at[item, me], target,
        )

    def arrived_out(item, origin):
        return remote(
            out_buf.at[item, origin], out_ref.at[origin * items + item],
            out_send.at[item, origin], out_recv.at[item, origin], origin,
        )

    def flipped(place, bit):
        return place + bit - 2 * bit * lax.rem(place // bit, 2)

    def masked(place, mask):
        for bit in bits:
            if mask & bit:
                place = flipped(place, bit)
        return place

    def grad_copy(item, which, message, landing=False):
        bit, mask = messages[message]
        target = flipped(me, bit)
        origin = masked(target if landing else me, mask)
        slot = grad_ref.at[origin * items + item, which]
        source = slot if mask and not landing else grad_buf.at[item, which]
        return remote(
            source, slot, grad_send.at[item, which, message], grad_recv.at[item, which, message],
            target,
        )

    def own_out(item):
        return pltpu.make_async_copy(
            out_buf.at[item, me], out_ref.at[me * items + item], own_sem.at[0, item]
        )

    def own_grad(item, which):
        return pltpu.make_async_copy(
            grad_buf.at[item, which], grad_ref.at[me * items + item, which],
            own_sem.at[1 + which, item],
        )

    def send_out(item):
        for distance in range(1, seqs):
            out_copy(item, peer(distance)).start()
        own_out(item).start()

    def send_chunk(item, index):
        for target in range(index * step, (index + 1) * step):

            @pl.when(target != me)
            def _():
                out_copy(item, target).start()

            @pl.when(target == me)
            def _():
                own_out(item).start()

    def grad_step(item, which, level):
        if level == 0:
            own_grad(item, which).start()
        for message, (bit, mask) in enumerate(messages):
            if level and bit == bits[level - 1]:
                grad_copy(item, which, message, True).wait_recv()
        for message, (bit, mask) in enumerate(messages):
            lowest = mask & -mask
            if lowest == (bits[level - 1] if level else 0):
                grad_copy(item, which, message).start()

    barrier = pltpu.get_barrier_semaphore()
    for distance in range(1, seqs):
        pl.semaphore_signal(
            barrier, inc=1, device_id={"seq": peer(distance)}, device_id_type=MESH
        )
    loads = [
        pltpu.make_async_copy(source, rows, load_sem.at[which])
        for which, (source, rows) in enumerate(((q_in, q_rows), (k_in, k_rows), (v_in, v_rows)))
    ]
    weights = (
        pltpu.make_async_copy(wq_ref.at[pl.ds(me * items, items)], wqs, weight_sem.at[0]),
        pltpu.make_async_copy(wk_ref.at[pl.ds(me * items, items)], wks, weight_sem.at[1]),
    )
    for copy in (*loads, *weights):
        copy.start()
    for copy, rows, by_head in zip(loads, (q_rows, k_rows, v_rows), (q_ref, k_ref, v_ref)):
        copy.wait()
        by_head[...] = jnp.transpose(rows[...], (1, 0, 2))
    for item in range(items):
        for which in range(3):
            own_input(which, item).start()
    pl.semaphore_wait(barrier, seqs - 1)
    for item in range(items):
        for which in range(3):
            for distance in range(1, seqs):
                input_copy(which, item, distance).start()
    for copy in weights:
        copy.wait()

    factor = math.log2(math.e) / math.sqrt(width)
    allowed = lax.broadcasted_iota(jnp.int32, (chunk, chunk), 1) <= lax.broadcasted_iota(
        jnp.int32, (chunk, chunk), 0
    )

    def rows_of(landing, item, start, count):
        return landing[item, start * step : (start + count) * step].reshape(count * chunk, width)

    def forward(item, index):
        query = rows_of(qs, item, index, 1)
        key = rows_of(ks, item, index, 1)
        value = rows_of(vs, item, index, 1)
        near = jnp.where(allowed, dot_nt(query, key), -1e30)
        top = jnp.max(near, -1, keepdims=True)
        if index:
            early_key = rows_of(ks, item, 0, index)
            early_value = rows_of(vs, item, 0, index)
            far = dot_nt(query, early_key)
            top = jnp.maximum(top, jnp.max(far, -1, keepdims=True))
        near = jnp.exp2((near - top) * factor)
        total = jnp.sum(near, -1, keepdims=True)
        summed = dot_nn(near.astype(jnp.bfloat16), value)
        if index:
            far = jnp.exp2((far - top) * factor)
            total = total + jnp.sum(far, -1, keepdims=True)
            summed = summed + dot_nn(far.astype(jnp.bfloat16), early_value)
        teacher = (summed * (1.0 / total)).astype(jnp.bfloat16).astype(jnp.float32)

        query_plus, query_minus = halves(query, wqs[item])
        key_plus, key_minus = halves(key, wks[item])
        query_feat = jnp.concatenate([query_plus, query_minus], -1).astype(jnp.bfloat16)
        key_feat = jnp.concatenate([key_plus, key_minus], -1).astype(jnp.bfloat16)
        rows = slice(index * chunk, (index + 1) * chunk)
        plus_k[rows] = key_plus
        minus_k[rows] = key_minus
        local = jnp.where(allowed, dot_nt(query_feat, key_feat), 0.0)
        numer = dot_nn(local.astype(jnp.bfloat16), value)
        denom = jnp.sum(local, -1, keepdims=True)
        query_wide = query_feat.astype(jnp.float32)
        if index:
            low = state[...].astype(jnp.bfloat16)
            sums = state_sum[...]
            numer = numer + dot_nn(query_feat, low)
            denom = denom + jnp.sum(query_wide * sums, -1, keepdims=True)
        inverse = 1.0 / denom
        student = numer * inverse
        out_buf[item, index * step : (index + 1) * step] = student.astype(jnp.bfloat16).reshape(
            step, block, width
        )
        diff = student - teacher
        grad_numer = (diff * inverse).astype(jnp.bfloat16)
        grad_denom = -jnp.sum(diff * student, -1, keepdims=True) * inverse
        link = jnp.where(allowed, dot_nt(grad_numer, value) + grad_denom, 0.0).astype(jnp.bfloat16)
        grad_query = dot_nn(link, key_feat)
        if index:
            grad_query = grad_query + dot_nt(grad_numer, low) + grad_denom * sums
        high, rest = two_terms(softmax_back(query_plus, query_minus, grad_query))
        term = dot_tn(query, high) + dot_tn(query, rest)
        grad_acc[0] = term if index == 0 else grad_acc[0] + term
        inner[rows] = dot_tn(link, query_feat)
        if index:
            back_state[index] = dot_tn(query_feat, grad_numer)
            back_sum[index] = jnp.sum(query_wide * grad_denom, 0, keepdims=True)
        if index + 1 < chunks:
            new_state = dot_tn(key_feat, value)
            new_sum = jnp.sum(key_feat.astype(jnp.float32), 0, keepdims=True)
            state[...] = new_state if index == 0 else state[...] + new_state
            state_sum[...] = new_sum if index == 0 else sums + new_sum

    def backward(item, index):
        last = index + 1 == chunks
        rows = slice(index * chunk, (index + 1) * chunk)
        grad_key = inner[rows]
        if not last:
            value = rows_of(vs, item, index, 1)
            newer = back_state[index + 1]
            newer_sum = back_sum[index + 1]
            if index + 2 < chunks:
                newer = newer + after[...]
                newer_sum = newer_sum + after_sum[...]
            if index:
                after[...] = newer
                after_sum[...] = newer_sum
            high, rest = two_terms(newer)
            grad_key = grad_key + dot_nt(value, high) + dot_nt(value, rest) + newer_sum
        high, rest = two_terms(softmax_back(plus_k[rows], minus_k[rows], grad_key))
        key = rows_of(ks, item, index, 1)
        term = dot_tn(key, high) + dot_tn(key, rest)
        grad_acc[1] = term if last else grad_acc[1] + term

    levels = len(bits)

    def one_head(item, carry):
        first, last = item > 0, item == items - 1
        for which in range(3):
            own_input(which, item).wait()
            for distance in range(1, seqs):
                arrived_input(which, item, distance).wait_recv()

        @pl.when(first)
        def _():
            for part in range(2):
                grad_step(item - 1, part, 0)
            send_out(item - 1)

        for index in range(chunks):
            forward(item, index)

        grad_buf[item, 0] = grad_acc[0].astype(jnp.bfloat16)
        for index in reversed(range(chunks)):
            backward(item, index)
            if index + 1 == chunks:

                @pl.when(first)
                def _():
                    for part in range(2):
                        grad_step(item - 1, part, 1)

                @pl.when(last)
                def _():
                    grad_step(item, 0, 0)

        grad_buf[item, 1] = grad_acc[1].astype(jnp.bfloat16)

        @pl.when(last)
        def _():
            grad_step(item, 1, 0)

        @pl.when(first)
        def _():
            for level in range(2, levels):
                for part in range(2):
                    grad_step(item - 1, part, level)

        return carry

    lax.fori_loop(0, items, one_head, 0)
    final = items - 1
    for level in range(1, levels):
        grad_step(final, 0, level)
        grad_step(final, 1, level)
        for index in range(chunks):
            if index % (levels - 1) == level - 1:
                send_chunk(final, index)
    for item in range(items):
        for which in range(3):
            for distance in range(1, seqs):
                input_copy(which, item, distance).wait_send()
        own_out(item).wait()
        for distance in range(1, seqs):
            out_copy(item, peer(distance)).wait_send()
            arrived_out(item, peer(distance)).wait_recv()
        for which in range(2):
            own_grad(item, which).wait()
            for message, (bit, mask) in enumerate(messages):
                grad_copy(item, which, message).wait_send()
                if bit == bits[-1]:
                    grad_copy(item, which, message, True).wait_recv()


def finish_kernel(
    out_ref, grad_ref, student_ref, query_ref, key_ref, by_head, rows, low, full, load_sem, store_sem
):
    heads = by_head.shape[0]
    part = heads // 2
    loads = [
        pltpu.make_async_copy(
            grad_ref.at[pl.ds(place * part, part)], low.at[pl.ds(place * part, part)],
            load_sem.at[place],
        )
        for place in range(2)
    ]
    loads.append(pltpu.make_async_copy(out_ref, by_head, load_sem.at[2]))
    for copy in loads:
        copy.start()
    stores = []
    for place in range(2):
        loads[place].wait()
        span = slice(place * part, (place + 1) * part)
        for which, target in enumerate((query_ref, key_ref)):
            full[which, span] = low[span, which].astype(jnp.float32)
            copy = pltpu.make_async_copy(
                full.at[which, pl.ds(place * part, part)], target.at[pl.ds(place * part, part)],
                store_sem.at[2 * place + which],
            )
            copy.start()
            stores.append(copy)
    loads[2].wait()
    rows[...] = jnp.transpose(by_head[...], (1, 0, 2))
    copy = pltpu.make_async_copy(rows, student_ref, store_sem.at[4])
    copy.start()
    stores.append(copy)
    for copy in stores:
        copy.wait()


def on_device(queries, keys, values, w_query, w_key):
    block, heads, width = queries.shape
    seqs = lax.axis_size("seq")
    if heads % seqs or seqs < 8 or seqs & (seqs - 1):
        return on_device_shared(queries, keys, values, w_query, w_key)
    items = heads // seqs
    length = seqs * block
    chunks = seqs // 2
    feat = 2 * width
    messages = len(doubling(seqs)[1])
    narrow, wide = jnp.bfloat16, jnp.float32
    sem = pltpu.SemaphoreType.DMA
    anywhere = pl.BlockSpec(memory_space=pl.ANY)
    out, grads = pl.pallas_call(
        functools.partial(fused_kernel, seqs, items),
        out_shape=(
            jax.ShapeDtypeStruct((heads, block, width), narrow),
            jax.ShapeDtypeStruct((heads, 2, width, width), narrow),
        ),
        in_specs=[anywhere] * 5,
        out_specs=(anywhere, anywhere),
        scratch_shapes=[
            pltpu.VMEM((block, heads, width), narrow),
            pltpu.VMEM((block, heads, width), narrow),
            pltpu.VMEM((block, heads, width), narrow),
            pltpu.VMEM((heads, block, width), narrow),
            pltpu.VMEM((heads, block, width), narrow),
            pltpu.VMEM((heads, block, width), narrow),
            pltpu.VMEM((items, seqs, block, width), narrow),
            pltpu.VMEM((items, seqs, block, width), narrow),
            pltpu.VMEM((items, seqs, block, width), narrow),
            pltpu.VMEM((items, width, width), narrow),
            pltpu.VMEM((items, width, width), narrow),
            pltpu.VMEM((length, width), wide),
            pltpu.VMEM((length, width), wide),
            pltpu.VMEM((8, feat), narrow),
            pltpu.VMEM((length, feat), wide),
            pltpu.VMEM((chunks, feat, width), wide),
            pltpu.VMEM((chunks, 1, feat), wide),
            pltpu.VMEM((feat, width), wide),
            pltpu.VMEM((1, feat), wide),
            pltpu.VMEM((feat, width), wide),
            pltpu.VMEM((1, feat), wide),
            pltpu.VMEM((2, width, width), wide),
            pltpu.VMEM((items, seqs, block, width), narrow),
            pltpu.VMEM((items, 2, width, width), narrow),
            sem((3, items, seqs)),
            sem((3, items, seqs)),
            sem((items, seqs)),
            sem((items, seqs)),
            sem((items, 2, messages)),
            sem((items, 2, messages)),
            sem((3, items)),
            sem((2,)),
            sem((3, items)),
            sem((3,)),
        ],
        compiler_params=pltpu.CompilerParams(
            collective_id=0, has_side_effects=True, vmem_limit_bytes=61 * 1024 * 1024
        ),
        name="transfer",
    )(
        queries,
        keys,
        values,
        w_query,
        w_key,
    )
    return pl.pallas_call(
        finish_kernel,
        out_shape=(
            jax.ShapeDtypeStruct((block, heads, width), narrow),
            jax.ShapeDtypeStruct((heads, width, width), wide),
            jax.ShapeDtypeStruct((heads, width, width), wide),
        ),
        in_specs=[anywhere] * 2,
        out_specs=(anywhere, anywhere, anywhere),
        scratch_shapes=[
            pltpu.VMEM((heads, block, width), narrow),
            pltpu.VMEM((block, heads, width), narrow),
            pltpu.VMEM((heads, 2, width, width), narrow),
            pltpu.VMEM((2, heads, width, width), wide),
            sem((1 + 2,)),
            sem((1 + 4,)),
        ],
        compiler_params=pltpu.CompilerParams(vmem_limit_bytes=61 * 1024 * 1024),
        name="finish",
    )(out, grads)


def solution(mesh):
    return jax.shard_map(
        on_device,
        mesh=mesh,
        in_specs=(
            P(("groups", "seq"), "heads", None),
            P(("groups", "seq"), "heads", None),
            P(("groups", "seq"), "heads", None),
            P("heads", None, None),
            P("heads", None, None),
        ),
        out_specs=(
            P(("groups", "seq"), "heads", None),
            P(("groups", "heads"), None, None),
            P(("groups", "heads"), None, None),
        ),
        check_vma=False,
    )
```

```python
import functools
import math

import jax
import jax.numpy as jnp
from jax import lax
from jax.experimental import pallas as pl
from jax.experimental.pallas import tpu as pltpu
from jax.sharding import PartitionSpec as P

HIGHEST = lax.Precision.HIGHEST


def passed_along(value, axis, steps):
    count = lax.axis_size(axis)
    pairs = [(source, (source + steps) % count) for source in range(count)]
    return lax.ppermute(value, axis, pairs)


def teacher_head(query, key_rows, value_rows, residue, spread):
    rows = query.shape[0]
    length = key_rows.shape[0]
    width = query.shape[1]
    query_block = min(512, rows)
    key_block = min(512, length)
    key_blocks = length // key_block
    scale = 1.0 / math.sqrt(width)

    def one_block(index):
        block_query = lax.dynamic_slice_in_dim(query, index * query_block, query_block, 0)
        position = (
            index * query_block + jnp.arange(query_block, dtype=jnp.int32)
        ) * spread + residue
        limit = (index + 1) * query_block * spread
        needed = jnp.minimum(key_blocks, (limit + key_block - 1) // key_block)

        def visit(inner, carry):
            top, total, summed = carry
            block_key = lax.dynamic_slice_in_dim(key_rows, inner * key_block, key_block, 0)
            block_value = lax.dynamic_slice_in_dim(value_rows, inner * key_block, key_block, 0)
            scores = (
                jnp.einsum("qd,kd->qk", block_query, block_key, preferred_element_type=jnp.float32)
                * scale
            )
            key_position = inner * key_block + jnp.arange(key_block, dtype=jnp.int32)
            scores = jnp.where(key_position[None, :] <= position[:, None], scores, -1e30)
            new_top = jnp.maximum(top, jnp.max(scores, 1))
            factor = jnp.exp(top - new_top)
            weights = jnp.exp(scores - new_top[:, None])
            total = total * factor + jnp.sum(weights, 1)
            summed = summed * factor[:, None] + jnp.dot(
                weights.astype(jnp.bfloat16), block_value, preferred_element_type=jnp.float32
            )
            return (new_top, total, summed)

        start = (
            jnp.full((query_block,), -1e30, jnp.float32),
            jnp.zeros((query_block,), jnp.float32),
            jnp.zeros((query_block, width), jnp.float32),
        )
        top, total, summed = lax.fori_loop(0, needed, visit, start)
        return (summed / total[:, None]).astype(jnp.bfloat16)

    blocks = lax.map(one_block, jnp.arange(rows // query_block, dtype=jnp.int32))
    return blocks.reshape(rows, width)


def feature_halves(inputs, weight):
    mixed = jnp.einsum("thd,hde->the", inputs, weight, preferred_element_type=jnp.float32)
    upper = jnp.exp(mixed)
    lower = jnp.exp(-mixed)
    return (upper / jnp.sum(upper, -1, keepdims=True), lower / jnp.sum(lower, -1, keepdims=True))


def feature_weight_grad(plus, minus, grad_feat, inputs):
    width = plus.shape[-1]
    grad_plus = grad_feat[..., :width]
    grad_minus = grad_feat[..., width:]
    grad_mixed = plus * (grad_plus - jnp.sum(plus * grad_plus, -1, keepdims=True))
    grad_mixed = grad_mixed - minus * (grad_minus - jnp.sum(minus * grad_minus, -1, keepdims=True))
    return jnp.einsum("thd,the->hde", inputs.astype(jnp.float32), grad_mixed, precision=HIGHEST)


def student_pass(query_feat, key_feat, values, teacher, allowed, states, sums):
    scores = jnp.einsum("nqhf,nkhf->nhqk", query_feat, key_feat, preferred_element_type=jnp.float32)
    scores = jnp.where(allowed, scores, 0.0)
    state_low = states.astype(jnp.bfloat16)
    numer = jnp.einsum(
        "nhqk,nkhd->nqhd", scores.astype(jnp.bfloat16), values, preferred_element_type=jnp.float32
    )
    numer = numer + jnp.einsum(
        "nqhf,nhfd->nqhd", query_feat, state_low, preferred_element_type=jnp.float32
    )
    denom = jnp.transpose(jnp.sum(scores, -1), (0, 2, 1)) + jnp.sum(
        query_feat.astype(jnp.float32) * sums[:, None], -1
    )
    student = numer / denom[..., None]
    diff = student - teacher.astype(jnp.float32)
    grad_numer = (diff / denom[..., None]).astype(jnp.bfloat16)
    grad_denom = -jnp.sum(diff * student, -1) / denom
    link = jnp.einsum("nqhd,nkhd->nhqk", grad_numer, values, preferred_element_type=jnp.float32)
    link = jnp.where(allowed, link + jnp.transpose(grad_denom, (0, 2, 1))[..., None], 0.0).astype(
        jnp.bfloat16
    )
    grad_query = jnp.einsum("nhqk,nkhf->nqhf", link, key_feat, preferred_element_type=jnp.float32)
    grad_query = grad_query + jnp.einsum(
        "nqhd,nhfd->nqhf", grad_numer, state_low, preferred_element_type=jnp.float32
    )
    grad_query = grad_query + grad_denom[..., None] * sums[:, None]
    back_state = jnp.einsum(
        "nqhf,nqhd->nhfd", query_feat, grad_numer, preferred_element_type=jnp.float32
    )
    back_sum = jnp.sum(query_feat.astype(jnp.float32) * grad_denom[..., None], 1)
    key_inner = jnp.einsum("nhqk,nqhf->nkhf", link, query_feat, preferred_element_type=jnp.float32)
    return (student, grad_query, key_inner, back_state, back_sum)


def on_device_shared(queries, keys, values, w_query, w_key):
    block, heads, width = queries.shape
    seqs = lax.axis_size("seq")
    here = lax.axis_index("seq")
    spread = max(1, seqs // heads)
    items = spread * heads // seqs
    residue = here * items // heads
    query_rows = queries.reshape(block // spread, spread * heads, width)
    key_rows = jnp.broadcast_to(keys[:, None], (block, spread, heads, width)).reshape(
        block, spread * heads, width
    )
    value_rows = jnp.broadcast_to(values[:, None], (block, spread, heads, width)).reshape(
        block, spread * heads, width
    )
    query_items, key_items, value_items = (
        lax.all_to_all(query_rows, "seq", split_axis=1, concat_axis=0, tiled=True),
        lax.all_to_all(key_rows, "seq", split_axis=1, concat_axis=0, tiled=True),
        lax.all_to_all(value_rows, "seq", split_axis=1, concat_axis=0, tiled=True),
    )

    def teach(group):
        return teacher_head(group[0], group[1], group[2], residue, spread)

    teacher_items = lax.map(
        teach,
        (
            jnp.moveaxis(query_items, 1, 0),
            jnp.moveaxis(key_items, 1, 0),
            jnp.moveaxis(value_items, 1, 0),
        ),
    )
    teacher_items = jnp.moveaxis(teacher_items, 0, 1)
    first = here * items % heads
    part_query = lax.dynamic_slice_in_dim(w_query, first, items, 0)
    part_key = lax.dynamic_slice_in_dim(w_key, first, items, 0)
    query_plus, query_minus = feature_halves(query_items, part_query)
    key_plus, key_minus = feature_halves(key_items, part_key)
    query_feat = jnp.concatenate([query_plus, query_minus], -1).astype(jnp.bfloat16)
    key_feat = jnp.concatenate([key_plus, key_minus], -1).astype(jnp.bfloat16)
    feat = 2 * width
    query_blocks = query_feat.reshape(seqs, block // spread, items, feat)
    key_blocks = key_feat.reshape(seqs, block, items, feat)
    value_blocks = value_items.reshape(seqs, block, items, width)
    teacher_blocks = teacher_items.reshape(seqs, block // spread, items, width)
    key_state = jnp.einsum(
        "nkhf,nkhd->nhfd", key_blocks, value_blocks, preferred_element_type=jnp.float32
    )
    key_sum = jnp.sum(key_blocks.astype(jnp.float32), 1)
    before_state = jnp.concatenate(
        [jnp.zeros_like(key_state[:1]), jnp.cumsum(key_state, 0)[:-1]], 0
    )
    before_sum = jnp.concatenate([jnp.zeros_like(key_sum[:1]), jnp.cumsum(key_sum, 0)[:-1]], 0)
    query_place = jnp.arange(block // spread, dtype=jnp.int32)
    key_place = jnp.arange(block, dtype=jnp.int32)
    allowed = key_place[None, :] <= query_place[:, None] * spread + residue
    student, grad_query, key_inner, back_state, back_sum = student_pass(
        query_blocks, key_blocks, value_blocks, teacher_blocks, allowed, before_state, before_sum
    )
    after_state = jnp.concatenate(
        [jnp.cumsum(back_state[::-1], 0)[::-1][1:], jnp.zeros_like(back_state[:1])], 0
    )
    after_sum = jnp.concatenate(
        [jnp.cumsum(back_sum[::-1], 0)[::-1][1:], jnp.zeros_like(back_sum[:1])], 0
    )
    grad_key = key_inner + jnp.einsum(
        "nkhd,nhfd->nkhf", value_blocks.astype(jnp.float32), after_state, precision=HIGHEST
    )
    grad_key = grad_key + after_sum[:, None]
    item_query_grad = feature_weight_grad(
        query_plus, query_minus, grad_query.reshape(-1, items, feat), query_items
    )
    item_key_grad = feature_weight_grad(
        key_plus, key_minus, grad_key.reshape(-1, items, feat), key_items
    )
    student_items = student.reshape(-1, items, width).astype(jnp.bfloat16)
    student_out = lax.all_to_all(
        student_items, "seq", split_axis=0, concat_axis=1, tiled=True
    ).reshape(block, heads, width)
    stride = seqs // spread
    summed_query = item_query_grad
    summed_key = item_key_grad
    for partner in range(1, spread):
        arrived = (
            passed_along(item_query_grad.astype(jnp.bfloat16), "seq", partner * stride).astype(
                item_query_grad.dtype
            ),
            passed_along(item_key_grad.astype(jnp.bfloat16), "seq", partner * stride).astype(
                item_key_grad.dtype
            ),
        )
        summed_query = summed_query + arrived[0]
        summed_key = summed_key + arrived[1]
    portion = width // spread
    owned_query = lax.dynamic_slice_in_dim(summed_query, residue * portion, portion, 1)[None]
    owned_key = lax.dynamic_slice_in_dim(summed_key, residue * portion, portion, 1)[None]
    whole_query, whole_key = (
        lax.all_gather(owned_query, "seq", axis=0, tiled=True),
        lax.all_gather(owned_key, "seq", axis=0, tiled=True),
    )

    def arrange(gathered):
        shaped = gathered.reshape(spread, stride, items, portion, width)
        return jnp.transpose(shaped, (1, 2, 0, 3, 4)).reshape(heads, width, width)

    query_grad = arrange(whole_query)
    key_grad = arrange(whole_key)
    return (student_out, query_grad, key_grad)


MESH = pl.DeviceIdType.MESH


def dot(left, right, dims):
    return lax.dot_general(left, right, (dims, ((), ())), preferred_element_type=jnp.float32)


def dot_nn(left, right):
    return dot(left, right, ((1,), (0,)))


def dot_nt(left, right):
    return dot(left, right, ((1,), (1,)))


def dot_tn(left, right):
    return dot(left, right, ((0,), (0,)))


def two_terms(value):
    high = value.astype(jnp.bfloat16)
    return high, (value - high.astype(jnp.float32)).astype(jnp.bfloat16)


def softmax_back(plus, minus, grad_feat):
    width = plus.shape[-1]
    grad_plus = grad_feat[:, :width]
    grad_minus = grad_feat[:, width:]
    mixed = plus * (grad_plus - jnp.sum(plus * grad_plus, -1, keepdims=True))
    return mixed - minus * (grad_minus - jnp.sum(minus * grad_minus, -1, keepdims=True))


def halves(rows, weight):
    mixed = dot_nn(rows, weight)
    upper = jnp.exp(mixed)
    lower = jnp.exp(-mixed)
    plus = upper * (1.0 / jnp.sum(upper, -1, keepdims=True))
    minus = lower * (1.0 / jnp.sum(lower, -1, keepdims=True))
    return plus, minus


def doubling(count):
    bits = [1 << place for place in reversed(range(count.bit_length() - 1))]
    messages = []
    for level, bit in enumerate(bits):
        masks = [0]
        for higher in bits[:level]:
            masks = masks + [mask + higher for mask in masks]
        messages = messages + [(bit, mask) for mask in masks]
    return bits, messages


def fused_kernel(
    seqs, items,
    q_in, k_in, v_in, wq_ref, wk_ref,
    out_ref, grad_ref,
    q_rows, k_rows, v_rows, q_ref, k_ref, v_ref, qs, ks, vs, wqs, wks, plus_k, minus_k, feat_k, inner, back_state, back_sum,
    state, state_sum, after, after_sum, grad_acc, out_buf, grad_buf,
    send_sem, recv_sem, out_send, out_recv, grad_send, grad_recv,
    local_sem, weight_sem, own_sem, load_sem,
):
    me = lax.axis_index("seq")
    block, width = q_ref.shape[1], q_ref.shape[2]
    step = 2
    chunk = block * step
    chunks = seqs // step
    feat = 2 * width
    bits, messages = doubling(seqs)

    def peer(distance):
        return lax.rem(me + distance, seqs)

    def remote(src, dst, send, recv, device):
        return pltpu.make_async_remote_copy(
            src_ref=src, dst_ref=dst, send_sem=send, recv_sem=recv,
            device_id={"seq": device}, device_id_type=MESH,
        )

    streams = ((q_ref, qs), (k_ref, ks), (v_ref, vs))

    def input_copy(which, item, distance):
        source, landing = streams[which]
        target = peer(distance)
        return remote(
            source.at[target * items + item], landing.at[item, me],
            send_sem.at[which, item, distance], recv_sem.at[which, item, distance], target,
        )

    def own_input(which, item):
        source, landing = streams[which]
        return pltpu.make_async_copy(
            source.at[me * items + item], landing.at[item, me], local_sem.at[which, item]
        )

    def arrived_input(which, item, distance):
        source, landing = streams[which]
        origin = peer(seqs - distance)
        return remote(
            source.at[item], landing.at[item, origin],
            send_sem.at[which, item, distance], recv_sem.at[which, item, distance], origin,
        )

    def out_copy(item, target):
        return remote(
            out_buf.at[item, target], out_ref.at[me * items + item],
            out_send.at[item, target], out_recv.at[item, me], target,
        )

    def arrived_out(item, origin):
        return remote(
            out_buf.at[item, origin], out_ref.at[origin * items + item],
            out_send.at[item, origin], out_recv.at[item, origin], origin,
        )

    def flipped(place, bit):
        return place + bit - 2 * bit * lax.rem(place // bit, 2)

    def masked(place, mask):
        for bit in bits:
            if mask & bit:
                place = flipped(place, bit)
        return place

    def grad_copy(item, which, message, landing=False):
        bit, mask = messages[message]
        target = flipped(me, bit)
        origin = masked(target if landing else me, mask)
        slot = grad_ref.at[origin * items + item, which]
        source = slot if mask and not landing else grad_buf.at[item, which]
        return remote(
            source, slot, grad_send.at[item, which, message], grad_recv.at[item, which, message],
            target,
        )

    def own_out(item):
        return pltpu.make_async_copy(
            out_buf.at[item, me], out_ref.at[me * items + item], own_sem.at[0, item]
        )

    def own_grad(item, which):
        return pltpu.make_async_copy(
            grad_buf.at[item, which], grad_ref.at[me * items + item, which],
            own_sem.at[1 + which, item],
        )

    def send_chunk(item, index, near):
        @pl.when(jnp.equal(me < seqs // 2, index < chunks // 2) == near)
        def _():
            for target in range(index * step, (index + 1) * step):

                @pl.when(target != me)
                def _():
                    out_copy(item, target).start()

                @pl.when(target == me)
                def _():
                    own_out(item).start()

    top = bits[0]

    def near_step(item, which, level):
        if level == 0:
            own_grad(item, which).start()
        for message, (bit, mask) in enumerate(messages):
            if level and bit == bits[level] and not mask & top:
                grad_copy(item, which, message, True).wait_recv()
        for message, (bit, mask) in enumerate(messages):
            if bit != top and not mask & top and mask & -mask == (bits[level] if level else 0):
                grad_copy(item, which, message).start()

    def far_step(item, which, level):
        if level == 0:
            grad_copy(item, which, 0).start()
            return
        for message, (bit, mask) in enumerate(messages):
            if bit == bits[level - 1] and (level == 1 or mask & top):
                grad_copy(item, which, message, True).wait_recv()
        for message, (bit, mask) in enumerate(messages):
            if mask & top and mask & -mask == bits[level - 1]:
                grad_copy(item, which, message).start()

    barrier = pltpu.get_barrier_semaphore()
    for distance in range(1, seqs):
        pl.semaphore_signal(
            barrier, inc=1, device_id={"seq": peer(distance)}, device_id_type=MESH
        )
    loads = [
        pltpu.make_async_copy(source, rows, load_sem.at[which])
        for which, (source, rows) in enumerate(((q_in, q_rows), (k_in, k_rows), (v_in, v_rows)))
    ]
    weights = (
        pltpu.make_async_copy(wq_ref.at[pl.ds(me * items, items)], wqs, weight_sem.at[0]),
        pltpu.make_async_copy(wk_ref.at[pl.ds(me * items, items)], wks, weight_sem.at[1]),
    )
    for copy in (*loads, *weights):
        copy.start()
    for copy, rows, by_head in zip(loads, (q_rows, k_rows, v_rows), (q_ref, k_ref, v_ref)):
        copy.wait()
        by_head[...] = jnp.transpose(rows[...], (1, 0, 2))
    for item in range(items):
        for which in range(3):
            own_input(which, item).start()
    pl.semaphore_wait(barrier, seqs - 1)
    for item in range(items):
        for which in range(3):
            for distance in sorted(range(1, seqs), key=lambda hops: abs(2 * hops - seqs)):
                input_copy(which, item, distance).start()
    for copy in weights:
        copy.wait()

    factor = math.log2(math.e) / math.sqrt(width)
    allowed = lax.broadcasted_iota(jnp.int32, (chunk, chunk), 1) <= lax.broadcasted_iota(
        jnp.int32, (chunk, chunk), 0
    )

    def rows_of(landing, item, start, count):
        return landing[item, start * step : (start + count) * step].reshape(count * chunk, width)

    def forward(item, index):
        query = rows_of(qs, item, index, 1)
        key = rows_of(ks, item, index, 1)
        value = rows_of(vs, item, index, 1)
        near = jnp.where(allowed, dot_nt(query, key), -1e30)
        top = jnp.max(near, -1, keepdims=True)
        if index:
            early_key = rows_of(ks, item, 0, index)
            early_value = rows_of(vs, item, 0, index)
            far = dot_nt(query, early_key)
            top = jnp.maximum(top, jnp.max(far, -1, keepdims=True))
        near = jnp.exp2((near - top) * factor)
        total = jnp.sum(near, -1, keepdims=True)
        summed = dot_nn(near.astype(jnp.bfloat16), value)
        if index:
            far = jnp.exp2((far - top) * factor)
            total = total + jnp.sum(far, -1, keepdims=True)
            summed = summed + dot_nn(far.astype(jnp.bfloat16), early_value)
        teacher = (summed * (1.0 / total)).astype(jnp.bfloat16).astype(jnp.float32)

        query_plus, query_minus = halves(query, wqs[item])
        key_plus, key_minus = halves(key, wks[item])
        query_feat = jnp.concatenate([query_plus, query_minus], -1).astype(jnp.bfloat16)
        key_feat = jnp.concatenate([key_plus, key_minus], -1).astype(jnp.bfloat16)
        rows = slice(index * chunk, (index + 1) * chunk)
        plus_k[rows] = key_plus
        minus_k[rows] = key_minus
        local = jnp.where(allowed, dot_nt(query_feat, key_feat), 0.0)
        numer = dot_nn(local.astype(jnp.bfloat16), value)
        denom = jnp.sum(local, -1, keepdims=True)
        query_wide = query_feat.astype(jnp.float32)
        if index:
            low = state[...].astype(jnp.bfloat16)
            sums = state_sum[...]
            numer = numer + dot_nn(query_feat, low)
            denom = denom + jnp.sum(query_wide * sums, -1, keepdims=True)
        inverse = 1.0 / denom
        student = numer * inverse
        out_buf[item, index * step : (index + 1) * step] = student.astype(jnp.bfloat16).reshape(
            step, block, width
        )
        diff = student - teacher
        grad_numer = (diff * inverse).astype(jnp.bfloat16)
        grad_denom = -jnp.sum(diff * student, -1, keepdims=True) * inverse
        link = jnp.where(allowed, dot_nt(grad_numer, value) + grad_denom, 0.0).astype(jnp.bfloat16)
        grad_query = dot_nn(link, key_feat)
        if index:
            grad_query = grad_query + dot_nt(grad_numer, low) + grad_denom * sums
        high, rest = two_terms(softmax_back(query_plus, query_minus, grad_query))
        term = dot_tn(query, high) + dot_tn(query, rest)
        grad_acc[0] = term if index == 0 else grad_acc[0] + term
        inner[rows] = dot_tn(link, query_feat)
        if index:
            back_state[index] = dot_tn(query_feat, grad_numer)
            back_sum[index] = jnp.sum(query_wide * grad_denom, 0, keepdims=True)
        if index + 1 < chunks:
            new_state = dot_tn(key_feat, value)
            new_sum = jnp.sum(key_feat.astype(jnp.float32), 0, keepdims=True)
            state[...] = new_state if index == 0 else state[...] + new_state
            state_sum[...] = new_sum if index == 0 else sums + new_sum

    def backward(item, index):
        last = index + 1 == chunks
        rows = slice(index * chunk, (index + 1) * chunk)
        grad_key = inner[rows]
        if not last:
            value = rows_of(vs, item, index, 1)
            newer = back_state[index + 1]
            newer_sum = back_sum[index + 1]
            if index + 2 < chunks:
                newer = newer + after[...]
                newer_sum = newer_sum + after_sum[...]
            if index:
                after[...] = newer
                after_sum[...] = newer_sum
            high, rest = two_terms(newer)
            grad_key = grad_key + dot_nt(value, high) + dot_nt(value, rest) + newer_sum
        high, rest = two_terms(softmax_back(plus_k[rows], minus_k[rows], grad_key))
        key = rows_of(ks, item, index, 1)
        term = dot_tn(key, high) + dot_tn(key, rest)
        grad_acc[1] = term if last else grad_acc[1] + term

    levels = len(bits)

    def one_head(item, carry):
        first, last = item > 0, item == items - 1
        for which in range(3):
            own_input(which, item).wait()
            for distance in range(1, seqs):
                arrived_input(which, item, distance).wait_recv()

        @pl.when(first)
        def _():
            for part in range(2):
                far_step(item - 1, part, 0)
            for index in range(chunks):
                send_chunk(item - 1, index, False)

        for index in range(chunks):
            forward(item, index)
            send_chunk(item, index, True)

        grad_buf[item, 0] = grad_acc[0].astype(jnp.bfloat16)
        for index in reversed(range(chunks)):
            backward(item, index)
            if index + 1 == chunks:

                @pl.when(first)
                def _():
                    for part in range(2):
                        far_step(item - 1, part, 1)

                @pl.when(last)
                def _():
                    near_step(item, 0, 0)
                    far_step(item, 0, 0)

        grad_buf[item, 1] = grad_acc[1].astype(jnp.bfloat16)

        @pl.when(last)
        def _():
            near_step(item, 1, 0)
            far_step(item, 1, 0)

        @pl.when(jnp.logical_not(last))
        def _():
            for part in range(2):
                near_step(item, part, 0)

        @pl.when(first)
        def _():
            for level in range(2, levels):
                for part in range(2):
                    far_step(item - 1, part, level)
                    near_step(item - 1, part, level - 1)

        return carry

    lax.fori_loop(0, items, one_head, 0)
    final = items - 1
    for level in range(1, levels):
        for part in range(2):
            far_step(final, part, level)
        if level < levels - 1:
            for part in range(2):
                near_step(final, part, level)
        for index in range(chunks):
            if index % (levels - 1) == level - 1:
                send_chunk(final, index, False)
    for item in range(items):
        for which in range(3):
            for distance in range(1, seqs):
                input_copy(which, item, distance).wait_send()
        own_out(item).wait()
        for distance in range(1, seqs):
            out_copy(item, peer(distance)).wait_send()
            arrived_out(item, peer(distance)).wait_recv()
        for which in range(2):
            own_grad(item, which).wait()
            for message, (bit, mask) in enumerate(messages):
                grad_copy(item, which, message).wait_send()
                if bit == bits[-1]:
                    grad_copy(item, which, message, True).wait_recv()


def finish_kernel(by_head, low, student_ref, query_ref, key_ref, rows, full, store_sem):
    heads = by_head.shape[0]
    part = heads // 2
    stores = []

    def store(source, target):
        copy = pltpu.make_async_copy(source, target, store_sem.at[len(stores)])
        copy.start()
        stores.append(copy)

    for place in range(2):
        span = pl.ds(place * part, part)
        for which, target in enumerate((query_ref, key_ref)):
            full[which, span] = low[span, which].astype(jnp.float32)
            store(full.at[which, span], target.at[span])
    rows[...] = jnp.transpose(by_head[...], (1, 0, 2))
    store(rows, student_ref)
    for copy in stores:
        copy.wait()


def on_device(queries, keys, values, w_query, w_key):
    block, heads, width = queries.shape
    seqs = lax.axis_size("seq")
    if heads % seqs or seqs < 8 or seqs & (seqs - 1):
        return on_device_shared(queries, keys, values, w_query, w_key)
    items = heads // seqs
    length = seqs * block
    chunks = seqs // 2
    feat = 2 * width
    messages = len(doubling(seqs)[1])
    narrow, wide = jnp.bfloat16, jnp.float32
    sem = pltpu.SemaphoreType.DMA
    anywhere = pl.BlockSpec(memory_space=pl.ANY)
    out, grads = pl.pallas_call(
        functools.partial(fused_kernel, seqs, items),
        out_shape=(
            jax.ShapeDtypeStruct((heads, block, width), narrow),
            jax.ShapeDtypeStruct((heads, 2, width, width), narrow),
        ),
        in_specs=[anywhere] * 5,
        out_specs=(anywhere, anywhere),
        scratch_shapes=[
            pltpu.VMEM((block, heads, width), narrow),
            pltpu.VMEM((block, heads, width), narrow),
            pltpu.VMEM((block, heads, width), narrow),
            pltpu.VMEM((heads, block, width), narrow),
            pltpu.VMEM((heads, block, width), narrow),
            pltpu.VMEM((heads, block, width), narrow),
            pltpu.VMEM((items, seqs, block, width), narrow),
            pltpu.VMEM((items, seqs, block, width), narrow),
            pltpu.VMEM((items, seqs, block, width), narrow),
            pltpu.VMEM((items, width, width), narrow),
            pltpu.VMEM((items, width, width), narrow),
            pltpu.VMEM((length, width), wide),
            pltpu.VMEM((length, width), wide),
            pltpu.VMEM((8, feat), narrow),
            pltpu.VMEM((length, feat), wide),
            pltpu.VMEM((chunks, feat, width), wide),
            pltpu.VMEM((chunks, 1, feat), wide),
            pltpu.VMEM((feat, width), wide),
            pltpu.VMEM((1, feat), wide),
            pltpu.VMEM((feat, width), wide),
            pltpu.VMEM((1, feat), wide),
            pltpu.VMEM((2, width, width), wide),
            pltpu.VMEM((items, seqs, block, width), narrow),
            pltpu.VMEM((items, 2, width, width), narrow),
            sem((3, items, seqs)),
            sem((3, items, seqs)),
            sem((items, seqs)),
            sem((items, seqs)),
            sem((items, 2, messages)),
            sem((items, 2, messages)),
            sem((3, items)),
            sem((2,)),
            sem((3, items)),
            sem((3,)),
        ],
        compiler_params=pltpu.CompilerParams(
            collective_id=0, has_side_effects=True, vmem_limit_bytes=48 * 1024 * 1024
        ),
        name="transfer",
    )(
        *(pltpu.with_memory_space_constraint(array, pltpu.HBM)
          for array in (queries, keys, values, w_query, w_key))
    )
    return pl.pallas_call(
        finish_kernel,
        out_shape=(
            jax.ShapeDtypeStruct((block, heads, width), narrow),
            jax.ShapeDtypeStruct((heads, width, width), wide),
            jax.ShapeDtypeStruct((heads, width, width), wide),
        ),
        in_specs=[pl.BlockSpec(memory_space=pltpu.VMEM)] * 2,
        out_specs=(anywhere, anywhere, anywhere),
        scratch_shapes=[
            pltpu.VMEM((block, heads, width), narrow),
            pltpu.VMEM((2, heads, width, width), wide),
            sem((1 + 4,)),
        ],
        compiler_params=pltpu.CompilerParams(vmem_limit_bytes=24 * 1024 * 1024),
        name="finish",
    )(out, grads)


def solution(mesh):
    return jax.shard_map(
        on_device,
        mesh=mesh,
        in_specs=(
            P(("groups", "seq"), "heads", None),
            P(("groups", "seq"), "heads", None),
            P(("groups", "seq"), "heads", None),
            P("heads", None, None),
            P("heads", None, None),
        ),
        out_specs=(
            P(("groups", "seq"), "heads", None),
            P(("groups", "heads"), None, None),
            P(("groups", "heads"), None, None),
        ),
        check_vma=False,
    )
```

```python
import functools
import math

import jax
import jax.numpy as jnp
from jax import lax
from jax.experimental import pallas as pl
from jax.experimental.pallas import tpu as pltpu
from jax.sharding import PartitionSpec as P

HIGHEST = lax.Precision.HIGHEST


def passed_along(value, axis, steps):
    count = lax.axis_size(axis)
    pairs = [(source, (source + steps) % count) for source in range(count)]
    return lax.ppermute(value, axis, pairs)


def teacher_head(query, key_rows, value_rows, residue, spread):
    rows = query.shape[0]
    length = key_rows.shape[0]
    width = query.shape[1]
    query_block = min(512, rows)
    key_block = min(512, length)
    key_blocks = length // key_block
    scale = 1.0 / math.sqrt(width)

    def one_block(index):
        block_query = lax.dynamic_slice_in_dim(query, index * query_block, query_block, 0)
        position = (
            index * query_block + jnp.arange(query_block, dtype=jnp.int32)
        ) * spread + residue
        limit = (index + 1) * query_block * spread
        needed = jnp.minimum(key_blocks, (limit + key_block - 1) // key_block)

        def visit(inner, carry):
            top, total, summed = carry
            block_key = lax.dynamic_slice_in_dim(key_rows, inner * key_block, key_block, 0)
            block_value = lax.dynamic_slice_in_dim(value_rows, inner * key_block, key_block, 0)
            scores = (
                jnp.einsum("qd,kd->qk", block_query, block_key, preferred_element_type=jnp.float32)
                * scale
            )
            key_position = inner * key_block + jnp.arange(key_block, dtype=jnp.int32)
            scores = jnp.where(key_position[None, :] <= position[:, None], scores, -1e30)
            new_top = jnp.maximum(top, jnp.max(scores, 1))
            factor = jnp.exp(top - new_top)
            weights = jnp.exp(scores - new_top[:, None])
            total = total * factor + jnp.sum(weights, 1)
            summed = summed * factor[:, None] + jnp.dot(
                weights.astype(jnp.bfloat16), block_value, preferred_element_type=jnp.float32
            )
            return (new_top, total, summed)

        start = (
            jnp.full((query_block,), -1e30, jnp.float32),
            jnp.zeros((query_block,), jnp.float32),
            jnp.zeros((query_block, width), jnp.float32),
        )
        top, total, summed = lax.fori_loop(0, needed, visit, start)
        return (summed / total[:, None]).astype(jnp.bfloat16)

    blocks = lax.map(one_block, jnp.arange(rows // query_block, dtype=jnp.int32))
    return blocks.reshape(rows, width)


def feature_halves(inputs, weight):
    mixed = jnp.einsum("thd,hde->the", inputs, weight, preferred_element_type=jnp.float32)
    upper = jnp.exp(mixed)
    lower = jnp.exp(-mixed)
    return (upper / jnp.sum(upper, -1, keepdims=True), lower / jnp.sum(lower, -1, keepdims=True))


def feature_weight_grad(plus, minus, grad_feat, inputs):
    width = plus.shape[-1]
    grad_plus = grad_feat[..., :width]
    grad_minus = grad_feat[..., width:]
    grad_mixed = plus * (grad_plus - jnp.sum(plus * grad_plus, -1, keepdims=True))
    grad_mixed = grad_mixed - minus * (grad_minus - jnp.sum(minus * grad_minus, -1, keepdims=True))
    return jnp.einsum("thd,the->hde", inputs.astype(jnp.float32), grad_mixed, precision=HIGHEST)


def student_pass(query_feat, key_feat, values, teacher, allowed, states, sums):
    scores = jnp.einsum("nqhf,nkhf->nhqk", query_feat, key_feat, preferred_element_type=jnp.float32)
    scores = jnp.where(allowed, scores, 0.0)
    state_low = states.astype(jnp.bfloat16)
    numer = jnp.einsum(
        "nhqk,nkhd->nqhd", scores.astype(jnp.bfloat16), values, preferred_element_type=jnp.float32
    )
    numer = numer + jnp.einsum(
        "nqhf,nhfd->nqhd", query_feat, state_low, preferred_element_type=jnp.float32
    )
    denom = jnp.transpose(jnp.sum(scores, -1), (0, 2, 1)) + jnp.sum(
        query_feat.astype(jnp.float32) * sums[:, None], -1
    )
    student = numer / denom[..., None]
    diff = student - teacher.astype(jnp.float32)
    grad_numer = (diff / denom[..., None]).astype(jnp.bfloat16)
    grad_denom = -jnp.sum(diff * student, -1) / denom
    link = jnp.einsum("nqhd,nkhd->nhqk", grad_numer, values, preferred_element_type=jnp.float32)
    link = jnp.where(allowed, link + jnp.transpose(grad_denom, (0, 2, 1))[..., None], 0.0).astype(
        jnp.bfloat16
    )
    grad_query = jnp.einsum("nhqk,nkhf->nqhf", link, key_feat, preferred_element_type=jnp.float32)
    grad_query = grad_query + jnp.einsum(
        "nqhd,nhfd->nqhf", grad_numer, state_low, preferred_element_type=jnp.float32
    )
    grad_query = grad_query + grad_denom[..., None] * sums[:, None]
    back_state = jnp.einsum(
        "nqhf,nqhd->nhfd", query_feat, grad_numer, preferred_element_type=jnp.float32
    )
    back_sum = jnp.sum(query_feat.astype(jnp.float32) * grad_denom[..., None], 1)
    key_inner = jnp.einsum("nhqk,nqhf->nkhf", link, query_feat, preferred_element_type=jnp.float32)
    return (student, grad_query, key_inner, back_state, back_sum)


def on_device_shared(queries, keys, values, w_query, w_key):
    block, heads, width = queries.shape
    seqs = lax.axis_size("seq")
    here = lax.axis_index("seq")
    spread = max(1, seqs // heads)
    items = spread * heads // seqs
    residue = here * items // heads
    query_rows = queries.reshape(block // spread, spread * heads, width)
    key_rows = jnp.broadcast_to(keys[:, None], (block, spread, heads, width)).reshape(
        block, spread * heads, width
    )
    value_rows = jnp.broadcast_to(values[:, None], (block, spread, heads, width)).reshape(
        block, spread * heads, width
    )
    query_items, key_items, value_items = (
        lax.all_to_all(query_rows, "seq", split_axis=1, concat_axis=0, tiled=True),
        lax.all_to_all(key_rows, "seq", split_axis=1, concat_axis=0, tiled=True),
        lax.all_to_all(value_rows, "seq", split_axis=1, concat_axis=0, tiled=True),
    )

    def teach(group):
        return teacher_head(group[0], group[1], group[2], residue, spread)

    teacher_items = lax.map(
        teach,
        (
            jnp.moveaxis(query_items, 1, 0),
            jnp.moveaxis(key_items, 1, 0),
            jnp.moveaxis(value_items, 1, 0),
        ),
    )
    teacher_items = jnp.moveaxis(teacher_items, 0, 1)
    first = here * items % heads
    part_query = lax.dynamic_slice_in_dim(w_query, first, items, 0)
    part_key = lax.dynamic_slice_in_dim(w_key, first, items, 0)
    query_plus, query_minus = feature_halves(query_items, part_query)
    key_plus, key_minus = feature_halves(key_items, part_key)
    query_feat = jnp.concatenate([query_plus, query_minus], -1).astype(jnp.bfloat16)
    key_feat = jnp.concatenate([key_plus, key_minus], -1).astype(jnp.bfloat16)
    feat = 2 * width
    query_blocks = query_feat.reshape(seqs, block // spread, items, feat)
    key_blocks = key_feat.reshape(seqs, block, items, feat)
    value_blocks = value_items.reshape(seqs, block, items, width)
    teacher_blocks = teacher_items.reshape(seqs, block // spread, items, width)
    key_state = jnp.einsum(
        "nkhf,nkhd->nhfd", key_blocks, value_blocks, preferred_element_type=jnp.float32
    )
    key_sum = jnp.sum(key_blocks.astype(jnp.float32), 1)
    before_state = jnp.concatenate(
        [jnp.zeros_like(key_state[:1]), jnp.cumsum(key_state, 0)[:-1]], 0
    )
    before_sum = jnp.concatenate([jnp.zeros_like(key_sum[:1]), jnp.cumsum(key_sum, 0)[:-1]], 0)
    query_place = jnp.arange(block // spread, dtype=jnp.int32)
    key_place = jnp.arange(block, dtype=jnp.int32)
    allowed = key_place[None, :] <= query_place[:, None] * spread + residue
    student, grad_query, key_inner, back_state, back_sum = student_pass(
        query_blocks, key_blocks, value_blocks, teacher_blocks, allowed, before_state, before_sum
    )
    after_state = jnp.concatenate(
        [jnp.cumsum(back_state[::-1], 0)[::-1][1:], jnp.zeros_like(back_state[:1])], 0
    )
    after_sum = jnp.concatenate(
        [jnp.cumsum(back_sum[::-1], 0)[::-1][1:], jnp.zeros_like(back_sum[:1])], 0
    )
    grad_key = key_inner + jnp.einsum(
        "nkhd,nhfd->nkhf", value_blocks.astype(jnp.float32), after_state, precision=HIGHEST
    )
    grad_key = grad_key + after_sum[:, None]
    item_query_grad = feature_weight_grad(
        query_plus, query_minus, grad_query.reshape(-1, items, feat), query_items
    )
    item_key_grad = feature_weight_grad(
        key_plus, key_minus, grad_key.reshape(-1, items, feat), key_items
    )
    student_items = student.reshape(-1, items, width).astype(jnp.bfloat16)
    student_out = lax.all_to_all(
        student_items, "seq", split_axis=0, concat_axis=1, tiled=True
    ).reshape(block, heads, width)
    stride = seqs // spread
    summed_query = item_query_grad
    summed_key = item_key_grad
    for partner in range(1, spread):
        arrived = (
            passed_along(item_query_grad.astype(jnp.bfloat16), "seq", partner * stride).astype(
                item_query_grad.dtype
            ),
            passed_along(item_key_grad.astype(jnp.bfloat16), "seq", partner * stride).astype(
                item_key_grad.dtype
            ),
        )
        summed_query = summed_query + arrived[0]
        summed_key = summed_key + arrived[1]
    portion = width // spread
    owned_query = lax.dynamic_slice_in_dim(summed_query, residue * portion, portion, 1)[None]
    owned_key = lax.dynamic_slice_in_dim(summed_key, residue * portion, portion, 1)[None]
    whole_query, whole_key = (
        lax.all_gather(owned_query, "seq", axis=0, tiled=True),
        lax.all_gather(owned_key, "seq", axis=0, tiled=True),
    )

    def arrange(gathered):
        shaped = gathered.reshape(spread, stride, items, portion, width)
        return jnp.transpose(shaped, (1, 2, 0, 3, 4)).reshape(heads, width, width)

    query_grad = arrange(whole_query)
    key_grad = arrange(whole_key)
    return (student_out, query_grad, key_grad)


MESH = pl.DeviceIdType.MESH


def dot(left, right, dims):
    return lax.dot_general(left, right, (dims, ((), ())), preferred_element_type=jnp.float32)


def dot_nn(left, right):
    return dot(left, right, ((1,), (0,)))


def dot_nt(left, right):
    return dot(left, right, ((1,), (1,)))


def dot_tn(left, right):
    return dot(left, right, ((0,), (0,)))


def two_terms(value):
    high = value.astype(jnp.bfloat16)
    return high, (value - high.astype(jnp.float32)).astype(jnp.bfloat16)


def softmax_back(plus, minus, grad_feat):
    width = plus.shape[-1]
    grad_plus = grad_feat[:, :width]
    grad_minus = grad_feat[:, width:]
    mixed = plus * (grad_plus - jnp.sum(plus * grad_plus, -1, keepdims=True))
    return mixed - minus * (grad_minus - jnp.sum(minus * grad_minus, -1, keepdims=True))


def halves(rows, weight):
    mixed = dot_nn(rows, weight)
    upper = jnp.exp(mixed)
    lower = jnp.exp(-mixed)
    plus = upper * (1.0 / jnp.sum(upper, -1, keepdims=True))
    minus = lower * (1.0 / jnp.sum(lower, -1, keepdims=True))
    return plus, minus


def doubling(count):
    bits = [1 << place for place in reversed(range(count.bit_length() - 1))]
    messages = []
    for level, bit in enumerate(bits):
        masks = [0]
        for higher in bits[:level]:
            masks = masks + [mask + higher for mask in masks]
        messages = messages + [(bit, mask) for mask in masks]
    return bits, messages


def fused_kernel(
    seqs, items,
    q_in, k_in, v_in, wq_ref, wk_ref,
    out_ref, grad_ref,
    q_rows, k_rows, v_rows, q_ref, k_ref, v_ref, qs, ks, vs, wqs, wks, plus_k, minus_k, feat_k, inner, back_state, back_sum,
    state, state_sum, after, after_sum, grad_acc, out_buf, grad_buf,
    send_sem, recv_sem, out_send, out_recv, grad_send, grad_recv,
    local_sem, weight_sem, own_sem, load_sem,
):
    me = lax.axis_index("seq")
    block, width = q_ref.shape[1], q_ref.shape[2]
    step = 2
    chunk = block * step
    chunks = seqs // step
    feat = 2 * width
    bits, messages = doubling(seqs)

    def peer(distance):
        return lax.rem(me + distance, seqs)

    def remote(src, dst, send, recv, device):
        return pltpu.make_async_remote_copy(
            src_ref=src, dst_ref=dst, send_sem=send, recv_sem=recv,
            device_id={"seq": device}, device_id_type=MESH,
        )

    streams = ((q_ref, qs), (k_ref, ks), (v_ref, vs))

    def input_copy(which, item, distance):
        source, landing = streams[which]
        target = peer(distance)
        return remote(
            source.at[target * items + item], landing.at[item, me],
            send_sem.at[which, item, distance], recv_sem.at[which, item, distance], target,
        )

    def own_input(which, item):
        source, landing = streams[which]
        return pltpu.make_async_copy(
            source.at[me * items + item], landing.at[item, me], local_sem.at[which, item]
        )

    def arrived_input(which, item, distance):
        source, landing = streams[which]
        origin = peer(seqs - distance)
        return remote(
            source.at[item], landing.at[item, origin],
            send_sem.at[which, item, distance], recv_sem.at[which, item, distance], origin,
        )

    def out_copy(item, target):
        return remote(
            out_buf.at[item, target], out_ref.at[me * items + item],
            out_send.at[item, target], out_recv.at[item, me], target,
        )

    def arrived_out(item, origin):
        return remote(
            out_buf.at[item, origin], out_ref.at[origin * items + item],
            out_send.at[item, origin], out_recv.at[item, origin], origin,
        )

    def flipped(place, bit):
        return place + bit - 2 * bit * lax.rem(place // bit, 2)

    def masked(place, mask):
        for bit in bits:
            if mask & bit:
                place = flipped(place, bit)
        return place

    def grad_copy(item, which, message, landing=False):
        bit, mask = messages[message]
        target = flipped(me, bit)
        origin = masked(target if landing else me, mask)
        slot = grad_ref.at[origin * items + item, which]
        source = slot if mask and not landing else grad_buf.at[item, which]
        return remote(
            source, slot, grad_send.at[item, which, message], grad_recv.at[item, which, message],
            target,
        )

    def own_out(item):
        return pltpu.make_async_copy(
            out_buf.at[item, me], out_ref.at[me * items + item], own_sem.at[0, item]
        )

    def own_grad(item, which):
        return pltpu.make_async_copy(
            grad_buf.at[item, which], grad_ref.at[me * items + item, which],
            own_sem.at[1 + which, item],
        )

    def send_chunk(item, index, near):
        @pl.when(jnp.equal(me < seqs // 2, index < chunks // 2) == near)
        def _():
            for target in range(index * step, (index + 1) * step):

                @pl.when(target != me)
                def _():
                    out_copy(item, target).start()

                @pl.when(target == me)
                def _():
                    own_out(item).start()

    top = bits[0]

    def near_step(item, which, level):
        if level == 0:
            own_grad(item, which).start()
        for message, (bit, mask) in enumerate(messages):
            if level and bit == bits[level] and not mask & top:
                grad_copy(item, which, message, True).wait_recv()
        for message, (bit, mask) in enumerate(messages):
            if bit != top and not mask & top and mask & -mask == (bits[level] if level else 0):
                grad_copy(item, which, message).start()

    def far_step(item, which, level):
        if level == 0:
            grad_copy(item, which, 0).start()
            return
        for message, (bit, mask) in enumerate(messages):
            if bit == bits[level - 1] and (level == 1 or mask & top):
                grad_copy(item, which, message, True).wait_recv()
        for message, (bit, mask) in enumerate(messages):
            if mask & top and mask & -mask == bits[level - 1]:
                grad_copy(item, which, message).start()

    barrier = pltpu.get_barrier_semaphore()
    for distance in range(1, seqs):
        pl.semaphore_signal(
            barrier, inc=1, device_id={"seq": peer(distance)}, device_id_type=MESH
        )
    loads = [
        pltpu.make_async_copy(source, rows, load_sem.at[which])
        for which, (source, rows) in enumerate(((q_in, q_rows), (k_in, k_rows), (v_in, v_rows)))
    ]
    weights = (
        pltpu.make_async_copy(wq_ref.at[pl.ds(me * items, items)], wqs, weight_sem.at[0]),
        pltpu.make_async_copy(wk_ref.at[pl.ds(me * items, items)], wks, weight_sem.at[1]),
    )
    for copy in (*loads, *weights):
        copy.start()
    for copy, rows, by_head in zip(loads, (q_rows, k_rows, v_rows), (q_ref, k_ref, v_ref)):
        copy.wait()
        by_head[...] = jnp.transpose(rows[...], (1, 0, 2))
    for item in range(items):
        for which in range(3):
            own_input(which, item).start()
    pl.semaphore_wait(barrier, seqs - 1)
    for item in range(items):
        for which in range(3):
            for distance in sorted(range(1, seqs), key=lambda hops: abs(2 * hops - seqs)):
                input_copy(which, item, distance).start()
    for copy in weights:
        copy.wait()

    factor = math.log2(math.e) / math.sqrt(width)
    allowed = lax.broadcasted_iota(jnp.int32, (chunk, chunk), 1) <= lax.broadcasted_iota(
        jnp.int32, (chunk, chunk), 0
    )

    def rows_of(landing, item, start, count):
        return landing[item, start * step : (start + count) * step].reshape(count * chunk, width)

    def forward(item, index):
        query = rows_of(qs, item, index, 1)
        key = rows_of(ks, item, index, 1)
        value = rows_of(vs, item, index, 1)
        near = jnp.where(allowed, dot_nt(query, key), -1e30)
        top = jnp.max(near, -1, keepdims=True)
        if index:
            early_key = rows_of(ks, item, 0, index)
            early_value = rows_of(vs, item, 0, index)
            far = dot_nt(query, early_key)
            top = jnp.maximum(top, jnp.max(far, -1, keepdims=True))
        near = jnp.exp2((near - top) * factor)
        total = jnp.sum(near, -1, keepdims=True)
        summed = dot_nn(near.astype(jnp.bfloat16), value)
        if index:
            far = jnp.exp2((far - top) * factor)
            total = total + jnp.sum(far, -1, keepdims=True)
            summed = summed + dot_nn(far.astype(jnp.bfloat16), early_value)
        teacher = (summed * (1.0 / total)).astype(jnp.bfloat16).astype(jnp.float32)

        query_plus, query_minus = halves(query, wqs[item])
        key_plus, key_minus = halves(key, wks[item])
        query_feat = jnp.concatenate([query_plus, query_minus], -1).astype(jnp.bfloat16)
        key_feat = jnp.concatenate([key_plus, key_minus], -1).astype(jnp.bfloat16)
        rows = slice(index * chunk, (index + 1) * chunk)
        plus_k[rows] = key_plus
        minus_k[rows] = key_minus
        local = jnp.where(allowed, dot_nt(query_feat, key_feat), 0.0)
        numer = dot_nn(local.astype(jnp.bfloat16), value)
        denom = jnp.sum(local, -1, keepdims=True)
        query_wide = query_feat.astype(jnp.float32)
        if index:
            low = state[...].astype(jnp.bfloat16)
            sums = state_sum[...]
            numer = numer + dot_nn(query_feat, low)
            denom = denom + jnp.sum(query_wide * sums, -1, keepdims=True)
        inverse = 1.0 / denom
        student = numer * inverse
        out_buf[item, index * step : (index + 1) * step] = student.astype(jnp.bfloat16).reshape(
            step, block, width
        )
        diff = student - teacher
        grad_numer = (diff * inverse).astype(jnp.bfloat16)
        grad_denom = -jnp.sum(diff * student, -1, keepdims=True) * inverse
        link = jnp.where(allowed, dot_nt(grad_numer, value) + grad_denom, 0.0).astype(jnp.bfloat16)
        grad_query = dot_nn(link, key_feat)
        if index:
            grad_query = grad_query + dot_nt(grad_numer, low) + grad_denom * sums
        high, rest = two_terms(softmax_back(query_plus, query_minus, grad_query))
        term = dot_tn(query, high) + dot_tn(query, rest)
        grad_acc[0] = term if index == 0 else grad_acc[0] + term
        inner[rows] = dot_tn(link, query_feat)
        if index:
            back_state[index] = dot_tn(query_feat, grad_numer)
            back_sum[index] = jnp.sum(query_wide * grad_denom, 0, keepdims=True)
        if index + 1 < chunks:
            new_state = dot_tn(key_feat, value)
            new_sum = jnp.sum(key_feat.astype(jnp.float32), 0, keepdims=True)
            state[...] = new_state if index == 0 else state[...] + new_state
            state_sum[...] = new_sum if index == 0 else sums + new_sum

    def backward(item, index):
        last = index + 1 == chunks
        rows = slice(index * chunk, (index + 1) * chunk)
        grad_key = inner[rows]
        if not last:
            value = rows_of(vs, item, index, 1)
            newer = back_state[index + 1]
            newer_sum = back_sum[index + 1]
            if index + 2 < chunks:
                newer = newer + after[...]
                newer_sum = newer_sum + after_sum[...]
            if index:
                after[...] = newer
                after_sum[...] = newer_sum
            high, rest = two_terms(newer)
            grad_key = grad_key + dot_nt(value, high) + dot_nt(value, rest) + newer_sum
        high, rest = two_terms(softmax_back(plus_k[rows], minus_k[rows], grad_key))
        key = rows_of(ks, item, index, 1)
        term = dot_tn(key, high) + dot_tn(key, rest)
        grad_acc[1] = term if last else grad_acc[1] + term

    levels = len(bits)

    def one_head(item, carry):
        first, last = item > 0, item == items - 1
        for which in range(3):
            own_input(which, item).wait()
            for distance in range(1, seqs):
                arrived_input(which, item, distance).wait_recv()

        @pl.when(first)
        def _():
            for part in range(2):
                far_step(item - 1, part, 0)
            for index in range(chunks):
                send_chunk(item - 1, index, False)

        for index in range(chunks):
            forward(item, index)
            send_chunk(item, index, True)

        grad_buf[item, 0] = grad_acc[0].astype(jnp.bfloat16)
        for index in reversed(range(chunks)):
            backward(item, index)
            if index + 1 == chunks:

                @pl.when(last)
                def _():
                    far_step(item, 0, 0)
                    near_step(item, 0, 0)

            if index == chunks // 2:

                @pl.when(first)
                def _():
                    for part in range(2):
                        far_step(item - 1, part, 1)

        grad_buf[item, 1] = grad_acc[1].astype(jnp.bfloat16)

        @pl.when(last)
        def _():
            far_step(item, 1, 0)
            near_step(item, 1, 0)

        @pl.when(jnp.logical_not(last))
        def _():
            for part in range(2):
                near_step(item, part, 0)

        @pl.when(first)
        def _():
            for level in range(2, levels):
                for part in range(2):
                    far_step(item - 1, part, level)
                    near_step(item - 1, part, level - 1)

        return carry

    lax.fori_loop(0, items, one_head, 0)
    final = items - 1
    for level in range(1, levels):
        for part in range(2):
            far_step(final, part, level)
        if level < levels - 1:
            for part in range(2):
                near_step(final, part, level)
        for index in range(chunks):
            if index % (levels - 1) == level - 1:
                send_chunk(final, index, False)
    for item in range(items):
        for which in range(3):
            for distance in range(1, seqs):
                input_copy(which, item, distance).wait_send()
        own_out(item).wait()
        for distance in range(1, seqs):
            out_copy(item, peer(distance)).wait_send()
            arrived_out(item, peer(distance)).wait_recv()
        for which in range(2):
            own_grad(item, which).wait()
            for message, (bit, mask) in enumerate(messages):
                grad_copy(item, which, message).wait_send()
                if bit == bits[-1]:
                    grad_copy(item, which, message, True).wait_recv()


def finish_kernel(by_head, low, student_ref, query_ref, key_ref, rows, full, store_sem):
    heads = by_head.shape[0]
    part = heads // 2
    stores = []

    def store(source, target):
        copy = pltpu.make_async_copy(source, target, store_sem.at[len(stores)])
        copy.start()
        stores.append(copy)

    for place in range(2):
        span = pl.ds(place * part, part)
        for which, target in enumerate((query_ref, key_ref)):
            full[which, span] = low[span, which].astype(jnp.float32)
            store(full.at[which, span], target.at[span])
    rows[...] = jnp.transpose(by_head[...], (1, 0, 2))
    store(rows, student_ref)
    for copy in stores:
        copy.wait()


def on_device(queries, keys, values, w_query, w_key):
    block, heads, width = queries.shape
    seqs = lax.axis_size("seq")
    if heads % seqs or seqs < 8 or seqs & (seqs - 1):
        return on_device_shared(queries, keys, values, w_query, w_key)
    items = heads // seqs
    length = seqs * block
    chunks = seqs // 2
    feat = 2 * width
    messages = len(doubling(seqs)[1])
    narrow, wide = jnp.bfloat16, jnp.float32
    sem = pltpu.SemaphoreType.DMA
    anywhere = pl.BlockSpec(memory_space=pl.ANY)
    out, grads = pl.pallas_call(
        functools.partial(fused_kernel, seqs, items),
        out_shape=(
            jax.ShapeDtypeStruct((heads, block, width), narrow),
            jax.ShapeDtypeStruct((heads, 2, width, width), narrow),
        ),
        in_specs=[anywhere] * 5,
        out_specs=(anywhere, anywhere),
        scratch_shapes=[
            pltpu.VMEM((block, heads, width), narrow),
            pltpu.VMEM((block, heads, width), narrow),
            pltpu.VMEM((block, heads, width), narrow),
            pltpu.VMEM((heads, block, width), narrow),
            pltpu.VMEM((heads, block, width), narrow),
            pltpu.VMEM((heads, block, width), narrow),
            pltpu.VMEM((items, seqs, block, width), narrow),
            pltpu.VMEM((items, seqs, block, width), narrow),
            pltpu.VMEM((items, seqs, block, width), narrow),
            pltpu.VMEM((items, width, width), narrow),
            pltpu.VMEM((items, width, width), narrow),
            pltpu.VMEM((length, width), wide),
            pltpu.VMEM((length, width), wide),
            pltpu.VMEM((8, feat), narrow),
            pltpu.VMEM((length, feat), wide),
            pltpu.VMEM((chunks, feat, width), wide),
            pltpu.VMEM((chunks, 1, feat), wide),
            pltpu.VMEM((feat, width), wide),
            pltpu.VMEM((1, feat), wide),
            pltpu.VMEM((feat, width), wide),
            pltpu.VMEM((1, feat), wide),
            pltpu.VMEM((2, width, width), wide),
            pltpu.VMEM((items, seqs, block, width), narrow),
            pltpu.VMEM((items, 2, width, width), narrow),
            sem((3, items, seqs)),
            sem((3, items, seqs)),
            sem((items, seqs)),
            sem((items, seqs)),
            sem((items, 2, messages)),
            sem((items, 2, messages)),
            sem((3, items)),
            sem((2,)),
            sem((3, items)),
            sem((3,)),
        ],
        compiler_params=pltpu.CompilerParams(
            collective_id=0, has_side_effects=True, vmem_limit_bytes=48 * 1024 * 1024
        ),
        name="transfer",
    )(
        *(pltpu.with_memory_space_constraint(array, pltpu.HBM)
          for array in (queries, keys, values, w_query, w_key))
    )
    return pl.pallas_call(
        finish_kernel,
        out_shape=(
            jax.ShapeDtypeStruct((block, heads, width), narrow),
            jax.ShapeDtypeStruct((heads, width, width), wide),
            jax.ShapeDtypeStruct((heads, width, width), wide),
        ),
        in_specs=[pl.BlockSpec(memory_space=pltpu.VMEM)] * 2,
        out_specs=(anywhere, anywhere, anywhere),
        scratch_shapes=[
            pltpu.VMEM((block, heads, width), narrow),
            pltpu.VMEM((2, heads, width, width), wide),
            sem((1 + 4,)),
        ],
        compiler_params=pltpu.CompilerParams(vmem_limit_bytes=24 * 1024 * 1024),
        name="finish",
    )(out, grads)


def solution(mesh):
    return jax.shard_map(
        on_device,
        mesh=mesh,
        in_specs=(
            P(("groups", "seq"), "heads", None),
            P(("groups", "seq"), "heads", None),
            P(("groups", "seq"), "heads", None),
            P("heads", None, None),
            P("heads", None, None),
        ),
        out_specs=(
            P(("groups", "seq"), "heads", None),
            P(("groups", "heads"), None, None),
            P(("groups", "heads"), None, None),
        ),
        check_vma=False,
    )
```

```python
import functools
import math

import jax
import jax.numpy as jnp
from jax import lax
from jax.experimental import pallas as pl
from jax.experimental.pallas import tpu as pltpu
from jax.sharding import PartitionSpec as P

HIGHEST = lax.Precision.HIGHEST


def passed_along(value, axis, steps):
    count = lax.axis_size(axis)
    pairs = [(source, (source + steps) % count) for source in range(count)]
    return lax.ppermute(value, axis, pairs)


def teacher_head(query, key_rows, value_rows, residue, spread):
    rows = query.shape[0]
    length = key_rows.shape[0]
    width = query.shape[1]
    query_block = min(512, rows)
    key_block = min(512, length)
    key_blocks = length // key_block
    scale = 1.0 / math.sqrt(width)

    def one_block(index):
        block_query = lax.dynamic_slice_in_dim(query, index * query_block, query_block, 0)
        position = (
            index * query_block + jnp.arange(query_block, dtype=jnp.int32)
        ) * spread + residue
        limit = (index + 1) * query_block * spread
        needed = jnp.minimum(key_blocks, (limit + key_block - 1) // key_block)

        def visit(inner, carry):
            top, total, summed = carry
            block_key = lax.dynamic_slice_in_dim(key_rows, inner * key_block, key_block, 0)
            block_value = lax.dynamic_slice_in_dim(value_rows, inner * key_block, key_block, 0)
            scores = (
                jnp.einsum("qd,kd->qk", block_query, block_key, preferred_element_type=jnp.float32)
                * scale
            )
            key_position = inner * key_block + jnp.arange(key_block, dtype=jnp.int32)
            scores = jnp.where(key_position[None, :] <= position[:, None], scores, -1e30)
            new_top = jnp.maximum(top, jnp.max(scores, 1))
            factor = jnp.exp(top - new_top)
            weights = jnp.exp(scores - new_top[:, None])
            total = total * factor + jnp.sum(weights, 1)
            summed = summed * factor[:, None] + jnp.dot(
                weights.astype(jnp.bfloat16), block_value, preferred_element_type=jnp.float32
            )
            return (new_top, total, summed)

        start = (
            jnp.full((query_block,), -1e30, jnp.float32),
            jnp.zeros((query_block,), jnp.float32),
            jnp.zeros((query_block, width), jnp.float32),
        )
        top, total, summed = lax.fori_loop(0, needed, visit, start)
        return (summed / total[:, None]).astype(jnp.bfloat16)

    blocks = lax.map(one_block, jnp.arange(rows // query_block, dtype=jnp.int32))
    return blocks.reshape(rows, width)


def feature_halves(inputs, weight):
    mixed = jnp.einsum("thd,hde->the", inputs, weight, preferred_element_type=jnp.float32)
    upper = jnp.exp(mixed)
    lower = jnp.exp(-mixed)
    return (upper / jnp.sum(upper, -1, keepdims=True), lower / jnp.sum(lower, -1, keepdims=True))


def feature_weight_grad(plus, minus, grad_feat, inputs):
    width = plus.shape[-1]
    grad_plus = grad_feat[..., :width]
    grad_minus = grad_feat[..., width:]
    grad_mixed = plus * (grad_plus - jnp.sum(plus * grad_plus, -1, keepdims=True))
    grad_mixed = grad_mixed - minus * (grad_minus - jnp.sum(minus * grad_minus, -1, keepdims=True))
    return jnp.einsum("thd,the->hde", inputs.astype(jnp.float32), grad_mixed, precision=HIGHEST)


def student_pass(query_feat, key_feat, values, teacher, allowed, states, sums):
    scores = jnp.einsum("nqhf,nkhf->nhqk", query_feat, key_feat, preferred_element_type=jnp.float32)
    scores = jnp.where(allowed, scores, 0.0)
    state_low = states.astype(jnp.bfloat16)
    numer = jnp.einsum(
        "nhqk,nkhd->nqhd", scores.astype(jnp.bfloat16), values, preferred_element_type=jnp.float32
    )
    numer = numer + jnp.einsum(
        "nqhf,nhfd->nqhd", query_feat, state_low, preferred_element_type=jnp.float32
    )
    denom = jnp.transpose(jnp.sum(scores, -1), (0, 2, 1)) + jnp.sum(
        query_feat.astype(jnp.float32) * sums[:, None], -1
    )
    student = numer / denom[..., None]
    diff = student - teacher.astype(jnp.float32)
    grad_numer = (diff / denom[..., None]).astype(jnp.bfloat16)
    grad_denom = -jnp.sum(diff * student, -1) / denom
    link = jnp.einsum("nqhd,nkhd->nhqk", grad_numer, values, preferred_element_type=jnp.float32)
    link = jnp.where(allowed, link + jnp.transpose(grad_denom, (0, 2, 1))[..., None], 0.0).astype(
        jnp.bfloat16
    )
    grad_query = jnp.einsum("nhqk,nkhf->nqhf", link, key_feat, preferred_element_type=jnp.float32)
    grad_query = grad_query + jnp.einsum(
        "nqhd,nhfd->nqhf", grad_numer, state_low, preferred_element_type=jnp.float32
    )
    grad_query = grad_query + grad_denom[..., None] * sums[:, None]
    back_state = jnp.einsum(
        "nqhf,nqhd->nhfd", query_feat, grad_numer, preferred_element_type=jnp.float32
    )
    back_sum = jnp.sum(query_feat.astype(jnp.float32) * grad_denom[..., None], 1)
    key_inner = jnp.einsum("nhqk,nqhf->nkhf", link, query_feat, preferred_element_type=jnp.float32)
    return (student, grad_query, key_inner, back_state, back_sum)


def on_device_shared(queries, keys, values, w_query, w_key):
    block, heads, width = queries.shape
    seqs = lax.axis_size("seq")
    here = lax.axis_index("seq")
    spread = max(1, seqs // heads)
    items = spread * heads // seqs
    residue = here * items // heads
    query_rows = queries.reshape(block // spread, spread * heads, width)
    key_rows = jnp.broadcast_to(keys[:, None], (block, spread, heads, width)).reshape(
        block, spread * heads, width
    )
    value_rows = jnp.broadcast_to(values[:, None], (block, spread, heads, width)).reshape(
        block, spread * heads, width
    )
    query_items, key_items, value_items = (
        lax.all_to_all(query_rows, "seq", split_axis=1, concat_axis=0, tiled=True),
        lax.all_to_all(key_rows, "seq", split_axis=1, concat_axis=0, tiled=True),
        lax.all_to_all(value_rows, "seq", split_axis=1, concat_axis=0, tiled=True),
    )

    def teach(group):
        return teacher_head(group[0], group[1], group[2], residue, spread)

    teacher_items = lax.map(
        teach,
        (
            jnp.moveaxis(query_items, 1, 0),
            jnp.moveaxis(key_items, 1, 0),
            jnp.moveaxis(value_items, 1, 0),
        ),
    )
    teacher_items = jnp.moveaxis(teacher_items, 0, 1)
    first = here * items % heads
    part_query = lax.dynamic_slice_in_dim(w_query, first, items, 0)
    part_key = lax.dynamic_slice_in_dim(w_key, first, items, 0)
    query_plus, query_minus = feature_halves(query_items, part_query)
    key_plus, key_minus = feature_halves(key_items, part_key)
    query_feat = jnp.concatenate([query_plus, query_minus], -1).astype(jnp.bfloat16)
    key_feat = jnp.concatenate([key_plus, key_minus], -1).astype(jnp.bfloat16)
    feat = 2 * width
    query_blocks = query_feat.reshape(seqs, block // spread, items, feat)
    key_blocks = key_feat.reshape(seqs, block, items, feat)
    value_blocks = value_items.reshape(seqs, block, items, width)
    teacher_blocks = teacher_items.reshape(seqs, block // spread, items, width)
    key_state = jnp.einsum(
        "nkhf,nkhd->nhfd", key_blocks, value_blocks, preferred_element_type=jnp.float32
    )
    key_sum = jnp.sum(key_blocks.astype(jnp.float32), 1)
    before_state = jnp.concatenate(
        [jnp.zeros_like(key_state[:1]), jnp.cumsum(key_state, 0)[:-1]], 0
    )
    before_sum = jnp.concatenate([jnp.zeros_like(key_sum[:1]), jnp.cumsum(key_sum, 0)[:-1]], 0)
    query_place = jnp.arange(block // spread, dtype=jnp.int32)
    key_place = jnp.arange(block, dtype=jnp.int32)
    allowed = key_place[None, :] <= query_place[:, None] * spread + residue
    student, grad_query, key_inner, back_state, back_sum = student_pass(
        query_blocks, key_blocks, value_blocks, teacher_blocks, allowed, before_state, before_sum
    )
    after_state = jnp.concatenate(
        [jnp.cumsum(back_state[::-1], 0)[::-1][1:], jnp.zeros_like(back_state[:1])], 0
    )
    after_sum = jnp.concatenate(
        [jnp.cumsum(back_sum[::-1], 0)[::-1][1:], jnp.zeros_like(back_sum[:1])], 0
    )
    grad_key = key_inner + jnp.einsum(
        "nkhd,nhfd->nkhf", value_blocks.astype(jnp.float32), after_state, precision=HIGHEST
    )
    grad_key = grad_key + after_sum[:, None]
    item_query_grad = feature_weight_grad(
        query_plus, query_minus, grad_query.reshape(-1, items, feat), query_items
    )
    item_key_grad = feature_weight_grad(
        key_plus, key_minus, grad_key.reshape(-1, items, feat), key_items
    )
    student_items = student.reshape(-1, items, width).astype(jnp.bfloat16)
    student_out = lax.all_to_all(
        student_items, "seq", split_axis=0, concat_axis=1, tiled=True
    ).reshape(block, heads, width)
    stride = seqs // spread
    summed_query = item_query_grad
    summed_key = item_key_grad
    for partner in range(1, spread):
        arrived = (
            passed_along(item_query_grad.astype(jnp.bfloat16), "seq", partner * stride).astype(
                item_query_grad.dtype
            ),
            passed_along(item_key_grad.astype(jnp.bfloat16), "seq", partner * stride).astype(
                item_key_grad.dtype
            ),
        )
        summed_query = summed_query + arrived[0]
        summed_key = summed_key + arrived[1]
    portion = width // spread
    owned_query = lax.dynamic_slice_in_dim(summed_query, residue * portion, portion, 1)[None]
    owned_key = lax.dynamic_slice_in_dim(summed_key, residue * portion, portion, 1)[None]
    whole_query, whole_key = (
        lax.all_gather(owned_query, "seq", axis=0, tiled=True),
        lax.all_gather(owned_key, "seq", axis=0, tiled=True),
    )

    def arrange(gathered):
        shaped = gathered.reshape(spread, stride, items, portion, width)
        return jnp.transpose(shaped, (1, 2, 0, 3, 4)).reshape(heads, width, width)

    query_grad = arrange(whole_query)
    key_grad = arrange(whole_key)
    return (student_out, query_grad, key_grad)


MESH = pl.DeviceIdType.MESH


def dot(left, right, dims):
    return lax.dot_general(left, right, (dims, ((), ())), preferred_element_type=jnp.float32)


def dot_nn(left, right):
    return dot(left, right, ((1,), (0,)))


def dot_nt(left, right):
    return dot(left, right, ((1,), (1,)))


def dot_tn(left, right):
    return dot(left, right, ((0,), (0,)))


def two_terms(value):
    high = value.astype(jnp.bfloat16)
    return high, (value - high.astype(jnp.float32)).astype(jnp.bfloat16)


def softmax_back(plus, minus, grad_feat):
    width = plus.shape[-1]
    grad_plus = grad_feat[:, :width]
    grad_minus = grad_feat[:, width:]
    mixed = plus * (grad_plus - jnp.sum(plus * grad_plus, -1, keepdims=True))
    return mixed - minus * (grad_minus - jnp.sum(minus * grad_minus, -1, keepdims=True))


def halves(rows, weight):
    mixed = dot_nn(rows, weight)
    upper = jnp.exp(mixed)
    lower = jnp.exp(-mixed)
    plus = upper * (1.0 / jnp.sum(upper, -1, keepdims=True))
    minus = lower * (1.0 / jnp.sum(lower, -1, keepdims=True))
    return plus, minus


def doubling(count):
    bits = [1 << place for place in reversed(range(count.bit_length() - 1))]
    messages = []
    for level, bit in enumerate(bits):
        masks = [0]
        for higher in bits[:level]:
            masks = masks + [mask + higher for mask in masks]
        messages = messages + [(bit, mask) for mask in masks]
    return bits, messages


def fused_kernel(
    seqs, items,
    q_in, k_in, v_in, wq_ref, wk_ref,
    out_ref, grad_ref,
    q_rows, k_rows, v_rows, q_ref, k_ref, v_ref, qs, ks, vs, wqs, wks, plus_k, minus_k, feat_k, inner, back_state, back_sum,
    state, state_sum, after, after_sum, grad_acc, out_buf, grad_buf,
    send_sem, recv_sem, out_send, out_recv, grad_send, grad_recv,
    local_sem, weight_sem, own_sem, load_sem,
):
    me = lax.axis_index("seq")
    block, width = q_ref.shape[1], q_ref.shape[2]
    step = 2
    chunk = block * step
    chunks = seqs // step
    feat = 2 * width
    bits, messages = doubling(seqs)

    def peer(distance):
        return lax.rem(me + distance, seqs)

    def remote(src, dst, send, recv, device):
        return pltpu.make_async_remote_copy(
            src_ref=src, dst_ref=dst, send_sem=send, recv_sem=recv,
            device_id={"seq": device}, device_id_type=MESH,
        )

    streams = ((q_ref, qs), (k_ref, ks), (v_ref, vs))

    def input_copy(which, item, distance):
        source, landing = streams[which]
        target = peer(distance)
        return remote(
            source.at[target * items + item], landing.at[item, me],
            send_sem.at[which, item, distance], recv_sem.at[which, item, distance], target,
        )

    def own_input(which, item):
        source, landing = streams[which]
        return pltpu.make_async_copy(
            source.at[me * items + item], landing.at[item, me], local_sem.at[which, item]
        )

    def arrived_input(which, item, distance):
        source, landing = streams[which]
        origin = peer(seqs - distance)
        return remote(
            source.at[item], landing.at[item, origin],
            send_sem.at[which, item, distance], recv_sem.at[which, item, distance], origin,
        )

    def out_copy(item, target):
        return remote(
            out_buf.at[item, target], out_ref.at[me * items + item],
            out_send.at[item, target], out_recv.at[item, me], target,
        )

    def arrived_out(item, origin):
        return remote(
            out_buf.at[item, origin], out_ref.at[origin * items + item],
            out_send.at[item, origin], out_recv.at[item, origin], origin,
        )

    def flipped(place, bit):
        return place + bit - 2 * bit * lax.rem(place // bit, 2)

    def masked(place, mask):
        for bit in bits:
            if mask & bit:
                place = flipped(place, bit)
        return place

    def grad_copy(item, which, message, landing=False):
        bit, mask = messages[message]
        target = flipped(me, bit)
        origin = masked(target if landing else me, mask)
        slot = grad_ref.at[origin * items + item, which]
        source = slot if mask and not landing else grad_buf.at[item, which]
        return remote(
            source, slot, grad_send.at[item, which, message], grad_recv.at[item, which, message],
            target,
        )

    def own_out(item):
        return pltpu.make_async_copy(
            out_buf.at[item, me], out_ref.at[me * items + item], own_sem.at[0, item]
        )

    def own_grad(item, which):
        return pltpu.make_async_copy(
            grad_buf.at[item, which], grad_ref.at[me * items + item, which],
            own_sem.at[1 + which, item],
        )

    def send_chunk(item, index, near):
        @pl.when(jnp.equal(me < seqs // 2, index < chunks // 2) == near)
        def _():
            for target in range(index * step, (index + 1) * step):

                @pl.when(target != me)
                def _():
                    out_copy(item, target).start()

                @pl.when(target == me)
                def _():
                    own_out(item).start()

    top = bits[0]

    def near_step(item, which, level):
        if level == 0:
            own_grad(item, which).start()
        for message, (bit, mask) in enumerate(messages):
            if level and bit == bits[level] and not mask & top:
                grad_copy(item, which, message, True).wait_recv()
        for message, (bit, mask) in enumerate(messages):
            if bit != top and not mask & top and mask & -mask == (bits[level] if level else 0):
                grad_copy(item, which, message).start()

    def far_step(item, which, level):
        if level == 0:
            grad_copy(item, which, 0).start()
            return
        for message, (bit, mask) in enumerate(messages):
            if bit == bits[level - 1] and (level == 1 or mask & top):
                grad_copy(item, which, message, True).wait_recv()
        for message, (bit, mask) in enumerate(messages):
            if mask & top and mask & -mask == bits[level - 1]:
                grad_copy(item, which, message).start()

    barrier = pltpu.get_barrier_semaphore()
    for distance in range(1, seqs):
        pl.semaphore_signal(
            barrier, inc=1, device_id={"seq": peer(distance)}, device_id_type=MESH
        )
    loads = [
        pltpu.make_async_copy(source, rows, load_sem.at[which])
        for which, (source, rows) in enumerate(((q_in, q_rows), (k_in, k_rows), (v_in, v_rows)))
    ]
    weights = (
        pltpu.make_async_copy(wq_ref.at[pl.ds(me * items, items)], wqs, weight_sem.at[0]),
        pltpu.make_async_copy(wk_ref.at[pl.ds(me * items, items)], wks, weight_sem.at[1]),
    )
    for copy in (*loads, *weights):
        copy.start()
    for copy, rows, by_head in zip(loads, (q_rows, k_rows, v_rows), (q_ref, k_ref, v_ref)):
        copy.wait()
        by_head[...] = jnp.transpose(rows[...], (1, 0, 2))
    for item in range(items):
        for which in range(3):
            own_input(which, item).start()
    pl.semaphore_wait(barrier, seqs - 1)
    for item in range(items):
        for which in range(3):
            for distance in sorted(range(1, seqs), key=lambda hops: abs(2 * hops - seqs)):
                input_copy(which, item, distance).start()
    for copy in weights:
        copy.wait()

    factor = math.log2(math.e) / math.sqrt(width)
    allowed = lax.broadcasted_iota(jnp.int32, (chunk, chunk), 1) <= lax.broadcasted_iota(
        jnp.int32, (chunk, chunk), 0
    )

    def rows_of(landing, item, start, count):
        return landing[item, start * step : (start + count) * step].reshape(count * chunk, width)

    def forward(item, index):
        query = rows_of(qs, item, index, 1)
        key = rows_of(ks, item, index, 1)
        value = rows_of(vs, item, index, 1)
        near = jnp.where(allowed, dot_nt(query, key), -1e30)
        top = jnp.max(near, -1, keepdims=True)
        if index:
            early_key = rows_of(ks, item, 0, index)
            early_value = rows_of(vs, item, 0, index)
            far = dot_nt(query, early_key)
            top = jnp.maximum(top, jnp.max(far, -1, keepdims=True))
        near = jnp.exp2((near - top) * factor)
        total = jnp.sum(near, -1, keepdims=True)
        summed = dot_nn(near.astype(jnp.bfloat16), value)
        if index:
            far = jnp.exp2((far - top) * factor)
            total = total + jnp.sum(far, -1, keepdims=True)
            summed = summed + dot_nn(far.astype(jnp.bfloat16), early_value)
        teacher = (summed * (1.0 / total)).astype(jnp.bfloat16).astype(jnp.float32)

        query_plus, query_minus = halves(query, wqs[item])
        key_plus, key_minus = halves(key, wks[item])
        query_feat = jnp.concatenate([query_plus, query_minus], -1).astype(jnp.bfloat16)
        key_feat = jnp.concatenate([key_plus, key_minus], -1).astype(jnp.bfloat16)
        rows = slice(index * chunk, (index + 1) * chunk)
        plus_k[rows] = key_plus
        minus_k[rows] = key_minus
        local = jnp.where(allowed, dot_nt(query_feat, key_feat), 0.0)
        numer = dot_nn(local.astype(jnp.bfloat16), value)
        denom = jnp.sum(local, -1, keepdims=True)
        query_wide = query_feat.astype(jnp.float32)
        if index:
            low = state[...].astype(jnp.bfloat16)
            sums = state_sum[...]
            numer = numer + dot_nn(query_feat, low)
            denom = denom + jnp.sum(query_wide * sums, -1, keepdims=True)
        inverse = 1.0 / denom
        student = numer * inverse
        out_buf[item, index * step : (index + 1) * step] = student.astype(jnp.bfloat16).reshape(
            step, block, width
        )
        diff = student - teacher
        grad_numer = (diff * inverse).astype(jnp.bfloat16)
        grad_denom = -jnp.sum(diff * student, -1, keepdims=True) * inverse
        link = jnp.where(allowed, dot_nt(grad_numer, value) + grad_denom, 0.0).astype(jnp.bfloat16)
        grad_query = dot_nn(link, key_feat)
        if index:
            grad_query = grad_query + dot_nt(grad_numer, low) + grad_denom * sums
        high, rest = two_terms(softmax_back(query_plus, query_minus, grad_query))
        term = dot_tn(query, high) + dot_tn(query, rest)
        grad_acc[0] = term if index == 0 else grad_acc[0] + term
        inner[rows] = dot_tn(link, query_feat)
        if index:
            back_state[index] = dot_tn(query_feat, grad_numer)
            back_sum[index] = jnp.sum(query_wide * grad_denom, 0, keepdims=True)
        if index + 1 < chunks:
            new_state = dot_tn(key_feat, value)
            new_sum = jnp.sum(key_feat.astype(jnp.float32), 0, keepdims=True)
            state[...] = new_state if index == 0 else state[...] + new_state
            state_sum[...] = new_sum if index == 0 else sums + new_sum

    def backward(item, index):
        last = index + 1 == chunks
        rows = slice(index * chunk, (index + 1) * chunk)
        grad_key = inner[rows]
        if not last:
            value = rows_of(vs, item, index, 1)
            newer = back_state[index + 1]
            newer_sum = back_sum[index + 1]
            if index + 2 < chunks:
                newer = newer + after[...]
                newer_sum = newer_sum + after_sum[...]
            if index:
                after[...] = newer
                after_sum[...] = newer_sum
            high, rest = two_terms(newer)
            grad_key = grad_key + dot_nt(value, high) + dot_nt(value, rest) + newer_sum
        high, rest = two_terms(softmax_back(plus_k[rows], minus_k[rows], grad_key))
        key = rows_of(ks, item, index, 1)
        term = dot_tn(key, high) + dot_tn(key, rest)
        grad_acc[1] = term if last else grad_acc[1] + term

    levels = len(bits)

    def one_head(item, carry):
        first, last = item > 0, item == items - 1
        for which in range(3):
            own_input(which, item).wait()
            for distance in range(1, seqs):
                arrived_input(which, item, distance).wait_recv()

        @pl.when(first)
        def _():
            for part in range(2):
                far_step(item - 1, part, 0)
            for index in range(chunks):
                send_chunk(item - 1, index, False)

        for index in range(chunks):
            forward(item, index)
            send_chunk(item, index, True)

        grad_buf[item, 0] = grad_acc[0].astype(jnp.bfloat16)
        for index in reversed(range(chunks)):
            backward(item, index)
            if index + 1 == chunks:

                @pl.when(last)
                def _():
                    far_step(item, 0, 0)
                    near_step(item, 0, 0)

            if index == chunks // 2:

                @pl.when(first)
                def _():
                    for part in range(2):
                        far_step(item - 1, part, 1)

        grad_buf[item, 1] = grad_acc[1].astype(jnp.bfloat16)

        @pl.when(last)
        def _():
            far_step(item, 1, 0)
            near_step(item, 1, 0)

        @pl.when(jnp.logical_not(last))
        def _():
            for part in range(2):
                near_step(item, part, 0)

        @pl.when(first)
        def _():
            for level in range(2, levels):
                for part in range(2):
                    far_step(item - 1, part, level)
                    near_step(item - 1, part, level - 1)

        return carry

    lax.fori_loop(0, items, one_head, 0)
    def settle_out(item):
        own_out(item).wait()
        for distance in range(1, seqs):
            out_copy(item, peer(distance)).wait_send()
            arrived_out(item, peer(distance)).wait_recv()

    final = items - 1
    for item in range(items):
        for which in range(3):
            for distance in range(1, seqs):
                input_copy(which, item, distance).wait_send()
    for level in range(1, levels):
        for part in range(2):
            far_step(final, part, level)
        if level < levels - 1:
            for part in range(2):
                near_step(final, part, level)
        for index in range(chunks):
            if index % (levels - 1) == level - 1:
                send_chunk(final, index, False)
        if level == 1:
            for item in range(final):
                settle_out(item)
    for item in range(items):
        if item == final:
            settle_out(item)
        for which in range(2):
            own_grad(item, which).wait()
            for message, (bit, mask) in enumerate(messages):
                grad_copy(item, which, message).wait_send()
                if bit == bits[-1]:
                    grad_copy(item, which, message, True).wait_recv()


def finish_kernel(by_head, low, student_ref, query_ref, key_ref, rows, full, store_sem):
    heads = by_head.shape[0]
    pieces = (store_sem.shape[0] - 1) // 2
    part = heads // pieces
    stores = []

    def store(source, target):
        copy = pltpu.make_async_copy(source, target, store_sem.at[len(stores)])
        copy.start()
        stores.append(copy)

    for place in range(pieces):
        span = pl.ds(place * part, part)
        for which, target in enumerate((query_ref, key_ref)):
            full[which, span] = low[span, which].astype(jnp.float32)
            store(full.at[which, span], target.at[span])
    rows[...] = jnp.transpose(by_head[...], (1, 0, 2))
    store(rows, student_ref)
    for copy in stores:
        copy.wait()


def on_device(queries, keys, values, w_query, w_key):
    block, heads, width = queries.shape
    seqs = lax.axis_size("seq")
    if heads % seqs or seqs < 8 or seqs & (seqs - 1):
        return on_device_shared(queries, keys, values, w_query, w_key)
    items = heads // seqs
    length = seqs * block
    chunks = seqs // 2
    feat = 2 * width
    messages = len(doubling(seqs)[1])
    narrow, wide = jnp.bfloat16, jnp.float32
    sem = pltpu.SemaphoreType.DMA
    anywhere = pl.BlockSpec(memory_space=pl.ANY)
    out, grads = pl.pallas_call(
        functools.partial(fused_kernel, seqs, items),
        out_shape=(
            jax.ShapeDtypeStruct((heads, block, width), narrow),
            jax.ShapeDtypeStruct((heads, 2, width, width), narrow),
        ),
        in_specs=[anywhere] * 5,
        out_specs=(anywhere, anywhere),
        scratch_shapes=[
            pltpu.VMEM((block, heads, width), narrow),
            pltpu.VMEM((block, heads, width), narrow),
            pltpu.VMEM((block, heads, width), narrow),
            pltpu.VMEM((heads, block, width), narrow),
            pltpu.VMEM((heads, block, width), narrow),
            pltpu.VMEM((heads, block, width), narrow),
            pltpu.VMEM((items, seqs, block, width), narrow),
            pltpu.VMEM((items, seqs, block, width), narrow),
            pltpu.VMEM((items, seqs, block, width), narrow),
            pltpu.VMEM((items, width, width), narrow),
            pltpu.VMEM((items, width, width), narrow),
            pltpu.VMEM((length, width), wide),
            pltpu.VMEM((length, width), wide),
            pltpu.VMEM((8, feat), narrow),
            pltpu.VMEM((length, feat), wide),
            pltpu.VMEM((chunks, feat, width), wide),
            pltpu.VMEM((chunks, 1, feat), wide),
            pltpu.VMEM((feat, width), wide),
            pltpu.VMEM((1, feat), wide),
            pltpu.VMEM((feat, width), wide),
            pltpu.VMEM((1, feat), wide),
            pltpu.VMEM((2, width, width), wide),
            pltpu.VMEM((items, seqs, block, width), narrow),
            pltpu.VMEM((items, 2, width, width), narrow),
            sem((3, items, seqs)),
            sem((3, items, seqs)),
            sem((items, seqs)),
            sem((items, seqs)),
            sem((items, 2, messages)),
            sem((items, 2, messages)),
            sem((3, items)),
            sem((2,)),
            sem((3, items)),
            sem((3,)),
        ],
        compiler_params=pltpu.CompilerParams(
            collective_id=0, has_side_effects=True, vmem_limit_bytes=48 * 1024 * 1024
        ),
        name="transfer",
    )(
        *(pltpu.with_memory_space_constraint(array, pltpu.HBM)
          for array in (queries, keys, values, w_query, w_key))
    )
    return pl.pallas_call(
        finish_kernel,
        out_shape=(
            jax.ShapeDtypeStruct((block, heads, width), narrow),
            jax.ShapeDtypeStruct((heads, width, width), wide),
            jax.ShapeDtypeStruct((heads, width, width), wide),
        ),
        in_specs=[pl.BlockSpec(memory_space=pltpu.VMEM)] * 2,
        out_specs=(anywhere, anywhere, anywhere),
        scratch_shapes=[
            pltpu.VMEM((block, heads, width), narrow),
            pltpu.VMEM((2, heads, width, width), wide),
            sem((1 + 2 * math.gcd(heads, 4),)),
        ],
        compiler_params=pltpu.CompilerParams(vmem_limit_bytes=24 * 1024 * 1024),
        name="finish",
    )(out, grads)


def solution(mesh):
    return jax.shard_map(
        on_device,
        mesh=mesh,
        in_specs=(
            P(("groups", "seq"), "heads", None),
            P(("groups", "seq"), "heads", None),
            P(("groups", "seq"), "heads", None),
            P("heads", None, None),
            P("heads", None, None),
        ),
        out_specs=(
            P(("groups", "seq"), "heads", None),
            P(("groups", "heads"), None, None),
            P(("groups", "heads"), None, None),
        ),
        check_vma=False,
    )
```

```python
import functools
import math

import jax
import jax.numpy as jnp
from jax import lax
from jax.experimental import pallas as pl
from jax.experimental.pallas import tpu as pltpu
from jax.sharding import PartitionSpec as P

HIGHEST = lax.Precision.HIGHEST


def passed_along(value, axis, steps):
    count = lax.axis_size(axis)
    pairs = [(source, (source + steps) % count) for source in range(count)]
    return lax.ppermute(value, axis, pairs)


def teacher_head(query, key_rows, value_rows, residue, spread):
    rows = query.shape[0]
    length = key_rows.shape[0]
    width = query.shape[1]
    query_block = min(512, rows)
    key_block = min(512, length)
    key_blocks = length // key_block
    scale = 1.0 / math.sqrt(width)

    def one_block(index):
        block_query = lax.dynamic_slice_in_dim(query, index * query_block, query_block, 0)
        position = (
            index * query_block + jnp.arange(query_block, dtype=jnp.int32)
        ) * spread + residue
        limit = (index + 1) * query_block * spread
        needed = jnp.minimum(key_blocks, (limit + key_block - 1) // key_block)

        def visit(inner, carry):
            top, total, summed = carry
            block_key = lax.dynamic_slice_in_dim(key_rows, inner * key_block, key_block, 0)
            block_value = lax.dynamic_slice_in_dim(value_rows, inner * key_block, key_block, 0)
            scores = (
                jnp.einsum("qd,kd->qk", block_query, block_key, preferred_element_type=jnp.float32)
                * scale
            )
            key_position = inner * key_block + jnp.arange(key_block, dtype=jnp.int32)
            scores = jnp.where(key_position[None, :] <= position[:, None], scores, -1e30)
            new_top = jnp.maximum(top, jnp.max(scores, 1))
            factor = jnp.exp(top - new_top)
            weights = jnp.exp(scores - new_top[:, None])
            total = total * factor + jnp.sum(weights, 1)
            summed = summed * factor[:, None] + jnp.dot(
                weights.astype(jnp.bfloat16), block_value, preferred_element_type=jnp.float32
            )
            return (new_top, total, summed)

        start = (
            jnp.full((query_block,), -1e30, jnp.float32),
            jnp.zeros((query_block,), jnp.float32),
            jnp.zeros((query_block, width), jnp.float32),
        )
        top, total, summed = lax.fori_loop(0, needed, visit, start)
        return (summed / total[:, None]).astype(jnp.bfloat16)

    blocks = lax.map(one_block, jnp.arange(rows // query_block, dtype=jnp.int32))
    return blocks.reshape(rows, width)


def feature_halves(inputs, weight):
    mixed = jnp.einsum("thd,hde->the", inputs, weight, preferred_element_type=jnp.float32)
    upper = jnp.exp(mixed)
    lower = jnp.exp(-mixed)
    return (upper / jnp.sum(upper, -1, keepdims=True), lower / jnp.sum(lower, -1, keepdims=True))


def feature_weight_grad(plus, minus, grad_feat, inputs):
    width = plus.shape[-1]
    grad_plus = grad_feat[..., :width]
    grad_minus = grad_feat[..., width:]
    grad_mixed = plus * (grad_plus - jnp.sum(plus * grad_plus, -1, keepdims=True))
    grad_mixed = grad_mixed - minus * (grad_minus - jnp.sum(minus * grad_minus, -1, keepdims=True))
    return jnp.einsum("thd,the->hde", inputs.astype(jnp.float32), grad_mixed, precision=HIGHEST)


def student_pass(query_feat, key_feat, values, teacher, allowed, states, sums):
    scores = jnp.einsum("nqhf,nkhf->nhqk", query_feat, key_feat, preferred_element_type=jnp.float32)
    scores = jnp.where(allowed, scores, 0.0)
    state_low = states.astype(jnp.bfloat16)
    numer = jnp.einsum(
        "nhqk,nkhd->nqhd", scores.astype(jnp.bfloat16), values, preferred_element_type=jnp.float32
    )
    numer = numer + jnp.einsum(
        "nqhf,nhfd->nqhd", query_feat, state_low, preferred_element_type=jnp.float32
    )
    denom = jnp.transpose(jnp.sum(scores, -1), (0, 2, 1)) + jnp.sum(
        query_feat.astype(jnp.float32) * sums[:, None], -1
    )
    student = numer / denom[..., None]
    diff = student - teacher.astype(jnp.float32)
    grad_numer = (diff / denom[..., None]).astype(jnp.bfloat16)
    grad_denom = -jnp.sum(diff * student, -1) / denom
    link = jnp.einsum("nqhd,nkhd->nhqk", grad_numer, values, preferred_element_type=jnp.float32)
    link = jnp.where(allowed, link + jnp.transpose(grad_denom, (0, 2, 1))[..., None], 0.0).astype(
        jnp.bfloat16
    )
    grad_query = jnp.einsum("nhqk,nkhf->nqhf", link, key_feat, preferred_element_type=jnp.float32)
    grad_query = grad_query + jnp.einsum(
        "nqhd,nhfd->nqhf", grad_numer, state_low, preferred_element_type=jnp.float32
    )
    grad_query = grad_query + grad_denom[..., None] * sums[:, None]
    back_state = jnp.einsum(
        "nqhf,nqhd->nhfd", query_feat, grad_numer, preferred_element_type=jnp.float32
    )
    back_sum = jnp.sum(query_feat.astype(jnp.float32) * grad_denom[..., None], 1)
    key_inner = jnp.einsum("nhqk,nqhf->nkhf", link, query_feat, preferred_element_type=jnp.float32)
    return (student, grad_query, key_inner, back_state, back_sum)


def on_device_shared(queries, keys, values, w_query, w_key):
    block, heads, width = queries.shape
    seqs = lax.axis_size("seq")
    here = lax.axis_index("seq")
    spread = max(1, seqs // heads)
    items = spread * heads // seqs
    residue = here * items // heads
    query_rows = queries.reshape(block // spread, spread * heads, width)
    key_rows = jnp.broadcast_to(keys[:, None], (block, spread, heads, width)).reshape(
        block, spread * heads, width
    )
    value_rows = jnp.broadcast_to(values[:, None], (block, spread, heads, width)).reshape(
        block, spread * heads, width
    )
    query_items, key_items, value_items = (
        lax.all_to_all(query_rows, "seq", split_axis=1, concat_axis=0, tiled=True),
        lax.all_to_all(key_rows, "seq", split_axis=1, concat_axis=0, tiled=True),
        lax.all_to_all(value_rows, "seq", split_axis=1, concat_axis=0, tiled=True),
    )

    def teach(group):
        return teacher_head(group[0], group[1], group[2], residue, spread)

    teacher_items = lax.map(
        teach,
        (
            jnp.moveaxis(query_items, 1, 0),
            jnp.moveaxis(key_items, 1, 0),
            jnp.moveaxis(value_items, 1, 0),
        ),
    )
    teacher_items = jnp.moveaxis(teacher_items, 0, 1)
    first = here * items % heads
    part_query = lax.dynamic_slice_in_dim(w_query, first, items, 0)
    part_key = lax.dynamic_slice_in_dim(w_key, first, items, 0)
    query_plus, query_minus = feature_halves(query_items, part_query)
    key_plus, key_minus = feature_halves(key_items, part_key)
    query_feat = jnp.concatenate([query_plus, query_minus], -1).astype(jnp.bfloat16)
    key_feat = jnp.concatenate([key_plus, key_minus], -1).astype(jnp.bfloat16)
    feat = 2 * width
    query_blocks = query_feat.reshape(seqs, block // spread, items, feat)
    key_blocks = key_feat.reshape(seqs, block, items, feat)
    value_blocks = value_items.reshape(seqs, block, items, width)
    teacher_blocks = teacher_items.reshape(seqs, block // spread, items, width)
    key_state = jnp.einsum(
        "nkhf,nkhd->nhfd", key_blocks, value_blocks, preferred_element_type=jnp.float32
    )
    key_sum = jnp.sum(key_blocks.astype(jnp.float32), 1)
    before_state = jnp.concatenate(
        [jnp.zeros_like(key_state[:1]), jnp.cumsum(key_state, 0)[:-1]], 0
    )
    before_sum = jnp.concatenate([jnp.zeros_like(key_sum[:1]), jnp.cumsum(key_sum, 0)[:-1]], 0)
    query_place = jnp.arange(block // spread, dtype=jnp.int32)
    key_place = jnp.arange(block, dtype=jnp.int32)
    allowed = key_place[None, :] <= query_place[:, None] * spread + residue
    student, grad_query, key_inner, back_state, back_sum = student_pass(
        query_blocks, key_blocks, value_blocks, teacher_blocks, allowed, before_state, before_sum
    )
    after_state = jnp.concatenate(
        [jnp.cumsum(back_state[::-1], 0)[::-1][1:], jnp.zeros_like(back_state[:1])], 0
    )
    after_sum = jnp.concatenate(
        [jnp.cumsum(back_sum[::-1], 0)[::-1][1:], jnp.zeros_like(back_sum[:1])], 0
    )
    grad_key = key_inner + jnp.einsum(
        "nkhd,nhfd->nkhf", value_blocks.astype(jnp.float32), after_state, precision=HIGHEST
    )
    grad_key = grad_key + after_sum[:, None]
    item_query_grad = feature_weight_grad(
        query_plus, query_minus, grad_query.reshape(-1, items, feat), query_items
    )
    item_key_grad = feature_weight_grad(
        key_plus, key_minus, grad_key.reshape(-1, items, feat), key_items
    )
    student_items = student.reshape(-1, items, width).astype(jnp.bfloat16)
    student_out = lax.all_to_all(
        student_items, "seq", split_axis=0, concat_axis=1, tiled=True
    ).reshape(block, heads, width)
    stride = seqs // spread
    summed_query = item_query_grad
    summed_key = item_key_grad
    for partner in range(1, spread):
        arrived = (
            passed_along(item_query_grad.astype(jnp.bfloat16), "seq", partner * stride).astype(
                item_query_grad.dtype
            ),
            passed_along(item_key_grad.astype(jnp.bfloat16), "seq", partner * stride).astype(
                item_key_grad.dtype
            ),
        )
        summed_query = summed_query + arrived[0]
        summed_key = summed_key + arrived[1]
    portion = width // spread
    owned_query = lax.dynamic_slice_in_dim(summed_query, residue * portion, portion, 1)[None]
    owned_key = lax.dynamic_slice_in_dim(summed_key, residue * portion, portion, 1)[None]
    whole_query, whole_key = (
        lax.all_gather(owned_query, "seq", axis=0, tiled=True),
        lax.all_gather(owned_key, "seq", axis=0, tiled=True),
    )

    def arrange(gathered):
        shaped = gathered.reshape(spread, stride, items, portion, width)
        return jnp.transpose(shaped, (1, 2, 0, 3, 4)).reshape(heads, width, width)

    query_grad = arrange(whole_query)
    key_grad = arrange(whole_key)
    return (student_out, query_grad, key_grad)


MESH = pl.DeviceIdType.MESH


def dot(left, right, dims):
    return lax.dot_general(left, right, (dims, ((), ())), preferred_element_type=jnp.float32)


def dot_nn(left, right):
    return dot(left, right, ((1,), (0,)))


def dot_nt(left, right):
    return dot(left, right, ((1,), (1,)))


def dot_tn(left, right):
    return dot(left, right, ((0,), (0,)))


def two_terms(value):
    high = value.astype(jnp.bfloat16)
    return high, (value - high.astype(jnp.float32)).astype(jnp.bfloat16)


def softmax_back(plus, minus, grad_feat):
    width = plus.shape[-1]
    grad_plus = grad_feat[:, :width]
    grad_minus = grad_feat[:, width:]
    mixed = plus * (grad_plus - jnp.sum(plus * grad_plus, -1, keepdims=True))
    return mixed - minus * (grad_minus - jnp.sum(minus * grad_minus, -1, keepdims=True))


def halves(rows, weight):
    mixed = dot_nn(rows, weight)
    upper = jnp.exp(mixed)
    lower = jnp.exp(-mixed)
    plus = upper * (1.0 / jnp.sum(upper, -1, keepdims=True))
    minus = lower * (1.0 / jnp.sum(lower, -1, keepdims=True))
    return plus, minus


def doubling(count):
    bits = [1 << place for place in reversed(range(count.bit_length() - 1))]
    messages = []
    for level, bit in enumerate(bits):
        masks = [0]
        for higher in bits[:level]:
            masks = masks + [mask + higher for mask in masks]
        messages = messages + [(bit, mask) for mask in masks]
    return bits, messages


def fused_kernel(
    seqs, items,
    q_in, k_in, v_in, wq_ref, wk_ref,
    out_ref, grad_ref,
    q_rows, k_rows, v_rows, q_ref, k_ref, v_ref, qs, ks, vs, wqs, wks, plus_k, minus_k, feat_k, inner, back_state, back_sum,
    state, state_sum, after, after_sum, grad_acc, out_buf, grad_buf,
    send_sem, recv_sem, out_send, out_recv, grad_send, grad_recv,
    local_sem, weight_sem, own_sem, load_sem,
):
    me = lax.axis_index("seq")
    block, width = q_ref.shape[1], q_ref.shape[2]
    step = 2
    chunk = block * step
    chunks = seqs // step
    feat = 2 * width
    bits, messages = doubling(seqs)

    def peer(distance):
        return lax.rem(me + distance, seqs)

    def remote(src, dst, send, recv, device):
        return pltpu.make_async_remote_copy(
            src_ref=src, dst_ref=dst, send_sem=send, recv_sem=recv,
            device_id={"seq": device}, device_id_type=MESH,
        )

    streams = ((q_ref, qs), (k_ref, ks), (v_ref, vs))

    def input_copy(which, item, distance):
        source, landing = streams[which]
        target = peer(distance)
        return remote(
            source.at[target * items + item], landing.at[item, me],
            send_sem.at[which, item, distance], recv_sem.at[which, item, distance], target,
        )

    def own_input(which, item):
        source, landing = streams[which]
        return pltpu.make_async_copy(
            source.at[me * items + item], landing.at[item, me], local_sem.at[which, item]
        )

    def arrived_input(which, item, distance):
        source, landing = streams[which]
        origin = peer(seqs - distance)
        return remote(
            source.at[item], landing.at[item, origin],
            send_sem.at[which, item, distance], recv_sem.at[which, item, distance], origin,
        )

    def out_copy(item, target):
        return remote(
            out_buf.at[item, target], out_ref.at[me * items + item],
            out_send.at[item, target], out_recv.at[item, me], target,
        )

    def arrived_out(item, origin):
        return remote(
            out_buf.at[item, origin], out_ref.at[origin * items + item],
            out_send.at[item, origin], out_recv.at[item, origin], origin,
        )

    def flipped(place, bit):
        return place + bit - 2 * bit * lax.rem(place // bit, 2)

    def masked(place, mask):
        for bit in bits:
            if mask & bit:
                place = flipped(place, bit)
        return place

    def grad_copy(item, which, message, landing=False):
        bit, mask = messages[message]
        target = flipped(me, bit)
        origin = masked(target if landing else me, mask)
        slot = grad_ref.at[origin * items + item, which]
        source = slot if mask and not landing else grad_buf.at[item, which]
        return remote(
            source, slot, grad_send.at[item, which, message], grad_recv.at[item, which, message],
            target,
        )

    def own_out(item):
        return pltpu.make_async_copy(
            out_buf.at[item, me], out_ref.at[me * items + item], own_sem.at[0, item]
        )

    def own_grad(item, which):
        return pltpu.make_async_copy(
            grad_buf.at[item, which], grad_ref.at[me * items + item, which],
            own_sem.at[1 + which, item],
        )

    def send_chunk(item, index, near):
        @pl.when(jnp.equal(me < seqs // 2, index < chunks // 2) == near)
        def _():
            for target in range(index * step, (index + 1) * step):

                @pl.when(target != me)
                def _():
                    out_copy(item, target).start()

                @pl.when(target == me)
                def _():
                    own_out(item).start()

    top = bits[0]

    def near_step(item, which, level):
        if level == 0:
            own_grad(item, which).start()
        for message, (bit, mask) in enumerate(messages):
            if level and bit == bits[level] and not mask & top:
                grad_copy(item, which, message, True).wait_recv()
        for message, (bit, mask) in enumerate(messages):
            if bit != top and not mask & top and mask & -mask == (bits[level] if level else 0):
                grad_copy(item, which, message).start()

    def far_step(item, which, level):
        if level == 0:
            grad_copy(item, which, 0).start()
            return
        for message, (bit, mask) in enumerate(messages):
            if bit == bits[level - 1] and (level == 1 or mask & top):
                grad_copy(item, which, message, True).wait_recv()
        for message, (bit, mask) in enumerate(messages):
            if mask & top and mask & -mask == bits[level - 1]:
                grad_copy(item, which, message).start()

    barrier = pltpu.get_barrier_semaphore()
    for distance in range(1, seqs):
        pl.semaphore_signal(
            barrier, inc=1, device_id={"seq": peer(distance)}, device_id_type=MESH
        )
    loads = [
        pltpu.make_async_copy(source, rows, load_sem.at[which])
        for which, (source, rows) in enumerate(((q_in, q_rows), (k_in, k_rows), (v_in, v_rows)))
    ]
    weights = (
        pltpu.make_async_copy(wq_ref.at[pl.ds(me * items, items)], wqs, weight_sem.at[0]),
        pltpu.make_async_copy(wk_ref.at[pl.ds(me * items, items)], wks, weight_sem.at[1]),
    )
    for copy in (*loads, *weights):
        copy.start()
    for copy, rows, by_head in zip(loads, (q_rows, k_rows, v_rows), (q_ref, k_ref, v_ref)):
        copy.wait()
        by_head[...] = jnp.transpose(rows[...], (1, 0, 2))
    pl.semaphore_wait(barrier, seqs - 1)
    for item in range(items):
        for which in range(3):
            for distance in sorted(range(1, seqs), key=lambda hops: abs(2 * hops - seqs)):
                input_copy(which, item, distance).start()
            own_input(which, item).start()
    for copy in weights:
        copy.wait()

    factor = math.log2(math.e) / math.sqrt(width)
    allowed = lax.broadcasted_iota(jnp.int32, (chunk, chunk), 1) <= lax.broadcasted_iota(
        jnp.int32, (chunk, chunk), 0
    )

    def rows_of(landing, item, start, count):
        return landing[item, start * step : (start + count) * step].reshape(count * chunk, width)

    def forward(item, index):
        query = rows_of(qs, item, index, 1)
        key = rows_of(ks, item, index, 1)
        value = rows_of(vs, item, index, 1)
        near = jnp.where(allowed, dot_nt(query, key), -1e30)
        top = jnp.max(near, -1, keepdims=True)
        if index:
            early_key = rows_of(ks, item, 0, index)
            early_value = rows_of(vs, item, 0, index)
            far = dot_nt(query, early_key)
            top = jnp.maximum(top, jnp.max(far, -1, keepdims=True))
        near = jnp.exp2((near - top) * factor)
        total = jnp.sum(near, -1, keepdims=True)
        summed = dot_nn(near.astype(jnp.bfloat16), value)
        if index:
            far = jnp.exp2((far - top) * factor)
            total = total + jnp.sum(far, -1, keepdims=True)
            summed = summed + dot_nn(far.astype(jnp.bfloat16), early_value)
        teacher = (summed * (1.0 / total)).astype(jnp.bfloat16).astype(jnp.float32)

        query_plus, query_minus = halves(query, wqs[item])
        key_plus, key_minus = halves(key, wks[item])
        query_feat = jnp.concatenate([query_plus, query_minus], -1).astype(jnp.bfloat16)
        key_feat = jnp.concatenate([key_plus, key_minus], -1).astype(jnp.bfloat16)
        rows = slice(index * chunk, (index + 1) * chunk)
        plus_k[rows] = key_plus
        minus_k[rows] = key_minus
        local = jnp.where(allowed, dot_nt(query_feat, key_feat), 0.0)
        numer = dot_nn(local.astype(jnp.bfloat16), value)
        denom = jnp.sum(local, -1, keepdims=True)
        query_wide = query_feat.astype(jnp.float32)
        if index:
            low = state[...].astype(jnp.bfloat16)
            sums = state_sum[...]
            numer = numer + dot_nn(query_feat, low)
            denom = denom + jnp.sum(query_wide * sums, -1, keepdims=True)
        inverse = 1.0 / denom
        student = numer * inverse
        out_buf[item, index * step : (index + 1) * step] = student.astype(jnp.bfloat16).reshape(
            step, block, width
        )
        diff = student - teacher
        grad_numer = (diff * inverse).astype(jnp.bfloat16)
        grad_denom = -jnp.sum(diff * student, -1, keepdims=True) * inverse
        link = jnp.where(allowed, dot_nt(grad_numer, value) + grad_denom, 0.0).astype(jnp.bfloat16)
        grad_query = dot_nn(link, key_feat)
        if index:
            grad_query = grad_query + dot_nt(grad_numer, low) + grad_denom * sums
        high, rest = two_terms(softmax_back(query_plus, query_minus, grad_query))
        term = dot_tn(query, high) + dot_tn(query, rest)
        grad_acc[0] = term if index == 0 else grad_acc[0] + term
        inner[rows] = dot_tn(link, query_feat)
        if index:
            back_state[index] = dot_tn(query_feat, grad_numer)
            back_sum[index] = jnp.sum(query_wide * grad_denom, 0, keepdims=True)
        if index + 1 < chunks:
            new_state = dot_tn(key_feat, value)
            new_sum = jnp.sum(key_feat.astype(jnp.float32), 0, keepdims=True)
            state[...] = new_state if index == 0 else state[...] + new_state
            state_sum[...] = new_sum if index == 0 else sums + new_sum

    def backward(item, index):
        last = index + 1 == chunks
        rows = slice(index * chunk, (index + 1) * chunk)
        grad_key = inner[rows]
        if not last:
            value = rows_of(vs, item, index, 1)
            newer = back_state[index + 1]
            newer_sum = back_sum[index + 1]
            if index + 2 < chunks:
                newer = newer + after[...]
                newer_sum = newer_sum + after_sum[...]
            if index:
                after[...] = newer
                after_sum[...] = newer_sum
            high, rest = two_terms(newer)
            grad_key = grad_key + dot_nt(value, high) + dot_nt(value, rest) + newer_sum
        high, rest = two_terms(softmax_back(plus_k[rows], minus_k[rows], grad_key))
        key = rows_of(ks, item, index, 1)
        term = dot_tn(key, high) + dot_tn(key, rest)
        grad_acc[1] = term if last else grad_acc[1] + term

    levels = len(bits)

    def one_head(item, carry):
        first, last = item > 0, item == items - 1
        for which in range(3):
            own_input(which, item).wait()
            for distance in range(1, seqs):
                arrived_input(which, item, distance).wait_recv()

        @pl.when(first)
        def _():
            for part in range(2):
                far_step(item - 1, part, 0)
            for index in range(chunks):
                send_chunk(item - 1, index, False)

        for index in range(chunks):
            forward(item, index)
            send_chunk(item, index, True)

        grad_buf[item, 0] = grad_acc[0].astype(jnp.bfloat16)
        for index in reversed(range(chunks)):
            backward(item, index)
            if index + 1 == chunks:

                @pl.when(last)
                def _():
                    far_step(item, 0, 0)
                    near_step(item, 0, 0)

            if index == chunks // 2:

                @pl.when(first)
                def _():
                    for part in range(2):
                        far_step(item - 1, part, 1)

        grad_buf[item, 1] = grad_acc[1].astype(jnp.bfloat16)

        @pl.when(last)
        def _():
            far_step(item, 1, 0)
            near_step(item, 1, 0)

        @pl.when(jnp.logical_not(last))
        def _():
            for part in range(2):
                near_step(item, part, 0)

        @pl.when(first)
        def _():
            for level in range(2, levels):
                for part in range(2):
                    far_step(item - 1, part, level)
                    near_step(item - 1, part, level - 1)

        return carry

    lax.fori_loop(0, items, one_head, 0)
    def settle_out(item):
        own_out(item).wait()
        for distance in range(1, seqs):
            out_copy(item, peer(distance)).wait_send()
            arrived_out(item, peer(distance)).wait_recv()

    final = items - 1
    for item in range(items):
        for which in range(3):
            for distance in range(1, seqs):
                input_copy(which, item, distance).wait_send()
    for level in range(1, levels):
        for part in range(2):
            far_step(final, part, level)
        if level < levels - 1:
            for part in range(2):
                near_step(final, part, level)
        for index in range(chunks):
            if index % (levels - 1) == level - 1:
                send_chunk(final, index, False)
        if level == 1:
            for item in range(final):
                settle_out(item)
    for item in range(items):
        if item == final:
            settle_out(item)
        for which in range(2):
            own_grad(item, which).wait()
            for message, (bit, mask) in enumerate(messages):
                grad_copy(item, which, message).wait_send()
                if bit == bits[-1]:
                    grad_copy(item, which, message, True).wait_recv()


def finish_kernel(by_head, low, student_ref, query_ref, key_ref, rows, full, store_sem):
    heads = by_head.shape[0]
    pieces = (store_sem.shape[0] - 1) // 2
    part = heads // pieces
    stores = []

    def store(source, target):
        copy = pltpu.make_async_copy(source, target, store_sem.at[len(stores)])
        copy.start()
        stores.append(copy)

    for place in range(pieces):
        span = pl.ds(place * part, part)
        for which, target in enumerate((query_ref, key_ref)):
            full[which, span] = low[span, which].astype(jnp.float32)
            store(full.at[which, span], target.at[span])
    rows[...] = jnp.transpose(by_head[...], (1, 0, 2))
    store(rows, student_ref)
    for copy in stores:
        copy.wait()


def on_device(queries, keys, values, w_query, w_key):
    block, heads, width = queries.shape
    seqs = lax.axis_size("seq")
    if heads % seqs or seqs < 8 or seqs & (seqs - 1):
        return on_device_shared(queries, keys, values, w_query, w_key)
    items = heads // seqs
    length = seqs * block
    chunks = seqs // 2
    feat = 2 * width
    messages = len(doubling(seqs)[1])
    narrow, wide = jnp.bfloat16, jnp.float32
    sem = pltpu.SemaphoreType.DMA
    anywhere = pl.BlockSpec(memory_space=pl.ANY)
    out, grads = pl.pallas_call(
        functools.partial(fused_kernel, seqs, items),
        out_shape=(
            jax.ShapeDtypeStruct((heads, block, width), narrow),
            jax.ShapeDtypeStruct((heads, 2, width, width), narrow),
        ),
        in_specs=[anywhere] * 5,
        out_specs=(anywhere, anywhere),
        scratch_shapes=[
            pltpu.VMEM((block, heads, width), narrow),
            pltpu.VMEM((block, heads, width), narrow),
            pltpu.VMEM((block, heads, width), narrow),
            pltpu.VMEM((heads, block, width), narrow),
            pltpu.VMEM((heads, block, width), narrow),
            pltpu.VMEM((heads, block, width), narrow),
            pltpu.VMEM((items, seqs, block, width), narrow),
            pltpu.VMEM((items, seqs, block, width), narrow),
            pltpu.VMEM((items, seqs, block, width), narrow),
            pltpu.VMEM((items, width, width), narrow),
            pltpu.VMEM((items, width, width), narrow),
            pltpu.VMEM((length, width), wide),
            pltpu.VMEM((length, width), wide),
            pltpu.VMEM((8, feat), narrow),
            pltpu.VMEM((length, feat), wide),
            pltpu.VMEM((chunks, feat, width), wide),
            pltpu.VMEM((chunks, 1, feat), wide),
            pltpu.VMEM((feat, width), wide),
            pltpu.VMEM((1, feat), wide),
            pltpu.VMEM((feat, width), wide),
            pltpu.VMEM((1, feat), wide),
            pltpu.VMEM((2, width, width), wide),
            pltpu.VMEM((items, seqs, block, width), narrow),
            pltpu.VMEM((items, 2, width, width), narrow),
            sem((3, items, seqs)),
            sem((3, items, seqs)),
            sem((items, seqs)),
            sem((items, seqs)),
            sem((items, 2, messages)),
            sem((items, 2, messages)),
            sem((3, items)),
            sem((2,)),
            sem((3, items)),
            sem((3,)),
        ],
        compiler_params=pltpu.CompilerParams(
            collective_id=0, has_side_effects=True, vmem_limit_bytes=48 * 1024 * 1024
        ),
        name="transfer",
    )(
        *(pltpu.with_memory_space_constraint(array, pltpu.HBM)
          for array in (queries, keys, values, w_query, w_key))
    )
    return pl.pallas_call(
        finish_kernel,
        out_shape=(
            jax.ShapeDtypeStruct((block, heads, width), narrow),
            jax.ShapeDtypeStruct((heads, width, width), wide),
            jax.ShapeDtypeStruct((heads, width, width), wide),
        ),
        in_specs=[pl.BlockSpec(memory_space=pltpu.VMEM)] * 2,
        out_specs=(anywhere, anywhere, anywhere),
        scratch_shapes=[
            pltpu.VMEM((block, heads, width), narrow),
            pltpu.VMEM((2, heads, width, width), wide),
            sem((1 + 2 * math.gcd(heads, 4),)),
        ],
        compiler_params=pltpu.CompilerParams(vmem_limit_bytes=24 * 1024 * 1024),
        name="finish",
    )(out, grads)


def solution(mesh):
    return jax.shard_map(
        on_device,
        mesh=mesh,
        in_specs=(
            P(("groups", "seq"), "heads", None),
            P(("groups", "seq"), "heads", None),
            P(("groups", "seq"), "heads", None),
            P("heads", None, None),
            P("heads", None, None),
        ),
        out_specs=(
            P(("groups", "seq"), "heads", None),
            P(("groups", "heads"), None, None),
            P(("groups", "heads"), None, None),
        ),
        check_vma=False,
    )
```
